512 devices in a mesh: req: 64 (over z, x), mp: 8 (over y, core).
Axes of the slice: x: 4, y: 4, z: 16, core: 2. Of those that a mesh axis runs over, the one named last changes fastest.
Arguments:
- queries: bfloat16 [16384, 2048], P('req', 'mp')
- keys: bfloat16 [16384, 1024], P('req', 'mp'), may hold values from -6 to 6
- values: bfloat16 [16384, 1024], P('req', 'mp'), may hold values from -6 to 6
- out_weight: bfloat16 [2048, 4608], P(None, 'mp'), may hold values from -0.125 to 0.125
- out_grad: bfloat16 [16384, 4608], P('req', 'mp'), may hold values from -6 to 6
- bank: float32 [16384, 2, 1024], P('req', None, 'mp'), may hold values from -6 to 6
- moment_one: float32 [16384, 2, 1024], P('req', None, 'mp')
- moment_two: float32 [16384, 2, 1024], P('req', None, 'mp'), as said below
- block_list: int32 [64, 32], replicated, may hold values from 0 to 127, as said below
- block_count: int32 [64], replicated, may hold values from 19 to 32, as said below
- token_count: int32 [64], P('req'), may hold values from 128 to 256, as said below
Outputs:
- attn_out: float32 [16384, 4608], P('req', 'mp')
- bank_next: float32 [16384, 2, 1024], P('req', None, 'mp')
- moment_next: float32 [16384, 2, 1024], P('req', None, 'mp')
- second_next: float32 [16384, 2, 1024], P('req', None, 'mp')
The draws below stay inside these ranges and needn't reach their ends.
Inputs may be any that keep to these rules, and one draw needn't show every extreme that they name: `block_list`: the 32 blocks of one request have distinct owners (block b belongs to owner b // 2). `block_count`: some request uses all 32 entries. The live tokens of a request are its first token_count[r] rows; some request fills all 256. `moment_two`: positive.
All inputs are finite; a program needn't handle non-finite values.
Results may differ from the reference program's by a relative error of at most 0.035.
Values may be sent and summed in bfloat16 or wider, within the bound.
A program may use at most 64 MiB of HBM per device.

```python
import math
import jax
import jax.numpy as jnp
from jax import lax

D = 4608
HEADS = 16
KV_HEADS = 8
HD = 128
BLOCK = 128
BLK_DEV = 2
TOK_DEV = 256
REQS = 64
TOKENS = 16384
BLOCKS = 128
VECTORS = 16384
MAXB = 32


def draw_queries(key, part):
    shape = (TOKENS, HEADS * HD)
    base_key, boost_key, offset_key = jax.random.split(jax.random.fold_in(key, 51), 3)
    period = max(TOK_DEV // 8, 2)
    position = jnp.arange(TOKENS, dtype=jnp.int32) % TOK_DEV
    offset = jnp.repeat(jax.random.randint(offset_key, (REQS,), 0, period), TOK_DEV)
    picked = position % period == offset
    boost = jax.random.uniform(boost_key, (TOKENS,), jnp.float32, 6.0, 12.0)
    base = jnp.clip(jax.random.normal(base_key, shape, jnp.float32), -6.0, 6.0)
    row_scale = jnp.ones((TOKENS,), jnp.float32)
    factor = jnp.where(picked, boost, row_scale)
    return (base * factor[:, None]).astype(jnp.bfloat16)


def draw_block_list(key, part):
    owner_total = BLOCKS // BLK_DEV
    score_key, pick_key = jax.random.split(jax.random.fold_in(key, 11))
    scores = jax.random.randint(score_key, (REQS, owner_total), 0, 1 << 20) * owner_total
    scores = scores + jnp.arange(owner_total, dtype=jnp.int32)[None, :]
    order = jnp.argsort(scores, axis=1, stable=True)[:, :MAXB].astype(jnp.int32)
    pick = jax.random.randint(pick_key, (REQS, MAXB), 0, BLK_DEV)
    return (order * BLK_DEV + pick).astype(jnp.int32)


def draw_block_count(key, part):
    least = MAXB * 3 // 5
    count_key, place_key = jax.random.split(jax.random.fold_in(key, 23))
    counts = jax.random.randint(count_key, (REQS,), least, MAXB + 1)
    place = jax.random.randint(place_key, (), 0, REQS)
    counts = counts.at[place].set(MAXB)
    counts = counts.at[(place + 1) % REQS].set(least)
    return counts.astype(jnp.int32)


def draw_token_count(key, part):
    least = TOK_DEV // 2
    count_key, place_key = jax.random.split(jax.random.fold_in(key, 37))
    counts = jax.random.randint(count_key, (REQS,), least, TOK_DEV + 1)
    place = jax.random.randint(place_key, (), 0, REQS)
    counts = counts.at[place].set(TOK_DEV)
    counts = counts.at[(place + 1) % REQS].set(least)
    return counts.astype(jnp.int32)


def gradient_scale():
    return 1.5 * math.sqrt(0.15 * BLOCKS * TOK_DEV) / (0.8 * MAXB * BLOCK + 0.5 * TOK_DEV)


def draw_moment_one(key, part):
    shape = (VECTORS, 2, KV_HEADS * HD)
    base = jax.random.normal(key, shape, jnp.float32)
    return base * gradient_scale()


def draw_moment_two(key, part):
    shape = (VECTORS, 2, KV_HEADS * HD)
    ratio = jnp.exp(jax.random.uniform(key, shape, jnp.float32, math.log(0.001), math.log(0.1)))
    return ratio * gradient_scale() * gradient_scale()


def shard_levels(key, dims, cuts, low, top_value):
    loudness, own = 1.0, jax.random.fold_in(key, 6)
    for dim, shards_of in cuts:
        steps = jnp.exp(jax.random.uniform(jax.random.fold_in(own, dim), (shards_of,), jnp.float32, low / len(cuts), top_value / len(cuts)))
        loudness = loudness * jnp.repeat(steps, dims[dim] // shards_of).reshape([-1 if axis == dim else 1 for axis in range(len(dims))])
    return loudness


def gaussian(stream_key, shape, scale, limit, pieces=(), kind=jnp.bfloat16):
    result = scale * jax.random.normal(stream_key, shape, jnp.float32)
    if pieces:
        result = result * shard_levels(stream_key, shape, pieces, -0.22, 0.18)
    return jnp.clip(result, -limit, limit).astype(kind)


def setup_inputs(seed: int = 0) -> dict:
    seeds = jax.random.split(jax.random.key(seed), 12)
    queries = draw_queries(jax.random.fold_in(seeds[11], 71), 0)
    keys = gaussian(seeds[1], (TOKENS, KV_HEADS * HD), 1.0, 6.0, ((0, 64), (1, 8)))
    values = gaussian(seeds[2], (TOKENS, KV_HEADS * HD), 1.0, 6.0, ((0, 64), (1, 8)))
    out_weight = gaussian(seeds[3], (HEADS * HD, D), (HEADS * HD) ** -0.5, 0.125, ((1, 8),))
    out_grad = gaussian(seeds[4], (TOKENS, D), 1.0, 6.0, ((0, 64), (1, 8)))
    bank = gaussian(seeds[5], (VECTORS, 2, KV_HEADS * HD), 1.0, 6.0, ((0, 64), (2, 8)), jnp.float32)
    moment_one = draw_moment_one(jax.random.fold_in(seeds[11], 71), 0)
    moment_two = draw_moment_two(jax.random.fold_in(seeds[11], 71), 0)
    block_list = draw_block_list(jax.random.fold_in(seeds[11], 71), 0)
    block_count = draw_block_count(jax.random.fold_in(seeds[11], 71), 0)
    token_count = draw_token_count(jax.random.fold_in(seeds[11], 71), 0)
    return dict(queries=queries, keys=keys, values=values, out_weight=out_weight, out_grad=out_grad, bank=bank, moment_one=moment_one, moment_two=moment_two, block_list=block_list, block_count=block_count, token_count=token_count)


softcap = 50.0
qscale = 1.0 / 12.0
beta_one = 0.9
beta_two = 0.999
learn_rate = 0.3
adam_eps = 1e-08
bias_one = 1.0 - 0.9 ** 10
bias_two = 1.0 - 0.999 ** 10

def capped(raw):
    return softcap * jnp.tanh(raw / softcap)

def rounded(value):
    return lax.optimization_barrier(value.astype(jnp.bfloat16)).astype(jnp.float32)

def reference(queries, keys, values, out_weight, out_grad, bank, moment_one, moment_two, block_list, block_count, token_count):
    group = HEADS // KV_HEADS
    bank_half = bank.astype(jnp.bfloat16).reshape(BLOCKS, BLOCK, 2, KV_HEADS * HD)
    position = jnp.arange(TOK_DEV, dtype=jnp.int32)
    causal = position[:, None] >= position[None, :]
    slot_block = jnp.arange(MAXB * BLOCK, dtype=jnp.int32) // BLOCK

    def request_step(grad_total, inputs):
        query_rows, key_rows, value_rows, grad_rows, listed, used_blocks, used_tokens = inputs
        query_four = query_rows.reshape(TOK_DEV, KV_HEADS, group, HD).astype(jnp.float32)
        key_three = key_rows.reshape(TOK_DEV, KV_HEADS, HD).astype(jnp.float32)
        value_three = value_rows.reshape(TOK_DEV, KV_HEADS, HD).astype(jnp.float32)
        prefix = bank_half[listed]
        prefix_keys = prefix[:, :, 0].reshape(MAXB * BLOCK, KV_HEADS, HD).astype(jnp.float32)
        prefix_values = prefix[:, :, 1].reshape(MAXB * BLOCK, KV_HEADS, HD).astype(jnp.float32)
        slot_ok = slot_block < used_blocks
        prefix_capped = capped(jnp.einsum('tkgd,skd->kgts', query_four, prefix_keys) * qscale)
        prefix_exp = jnp.where(slot_ok, jnp.exp(prefix_capped), 0.0)
        token_capped = capped(jnp.einsum('tkgd,skd->kgts', query_four, key_three) * qscale)
        token_exp = jnp.where(causal, jnp.exp(token_capped), 0.0)
        denominator = lax.optimization_barrier(jnp.sum(prefix_exp, axis=-1)) + lax.optimization_barrier(jnp.sum(token_exp, axis=-1))
        prefix_prob = prefix_exp / denominator[..., None]
        prefix_weights = rounded(prefix_prob)
        token_weights = rounded(token_exp / denominator[..., None])
        mixed = jnp.einsum('kgts,skd->tkgd', prefix_weights, prefix_values) + jnp.einsum('kgts,skd->tkgd', token_weights, value_three)
        row_ok = position[:, None] < used_tokens
        heads_out = jnp.where(row_ok, mixed.reshape(TOK_DEV, HEADS * HD), 0.0).astype(jnp.bfloat16)
        out_rows = jnp.dot(heads_out, out_weight, preferred_element_type=jnp.float32)
        head_grad = jnp.dot(grad_rows, out_weight.T, preferred_element_type=jnp.float32)
        grad_heads = rounded(jnp.where(row_ok, head_grad, 0.0)).reshape(TOK_DEV, KV_HEADS, group, HD)
        heads_four = heads_out.astype(jnp.float32).reshape(TOK_DEV, KV_HEADS, group, HD)
        delta = jnp.einsum('tkgd,tkgd->kgt', grad_heads, heads_four)
        dprob = jnp.einsum('tkgd,skd->kgts', grad_heads, prefix_values)
        dscore = rounded(prefix_prob * (dprob - delta[..., None]) * (1.0 - (prefix_capped / softcap) ** 2) * qscale)
        key_grad = jnp.einsum('kgts,tkgd->skd', dscore, query_four)
        value_grad = jnp.einsum('kgts,tkgd->skd', prefix_weights, grad_heads)
        block_grad = jnp.stack((key_grad.reshape(MAXB, BLOCK, KV_HEADS * HD), value_grad.reshape(MAXB, BLOCK, KV_HEADS * HD)), axis=2)
        return (grad_total.at[listed].add(block_grad), out_rows)
    inputs = (queries.reshape(REQS, TOK_DEV, HEADS * HD), keys.reshape(REQS, TOK_DEV, KV_HEADS * HD), values.reshape(REQS, TOK_DEV, KV_HEADS * HD), out_grad.reshape(REQS, TOK_DEV, D), block_list, block_count, token_count)
    start_grad = jnp.zeros((BLOCKS, BLOCK, 2, KV_HEADS * HD), jnp.float32)
    grad_total, out_rows = lax.scan(request_step, start_grad, inputs)
    attn_out = out_rows.reshape(REQS * TOK_DEV, D)
    grad = grad_total.reshape(VECTORS, 2, KV_HEADS * HD)
    moment_next = beta_one * moment_one + (1.0 - beta_one) * grad
    second_next = beta_two * moment_two + (1.0 - beta_two) * grad * grad
    bank_next = bank - learn_rate * (moment_next / bias_one) / (jnp.sqrt(second_next / bias_two) + adam_eps)
    return (attn_out, bank_next, moment_next, second_next)
```

```python
import functools

import jax
import jax.numpy as jnp
from jax import lax
from jax.experimental import pallas as pl
from jax.experimental.pallas import tpu as pltpu
from jax.sharding import PartitionSpec as P

HD = 128
BLOCK = 128
KEY, VALUE = 0, 1
RIGHT, LEFT = 0, 1

softcap = 50.0
qscale = 1.0 / 12.0
beta_one = 0.9
beta_two = 0.999
learn_rate = 0.3
adam_eps = 1e-08
bias_one = 1.0 - 0.9**10
bias_two = 1.0 - 0.999**10

NN = (((1,), (0,)), ((), ()))
NT = (((1,), (1,)), ((), ()))
TN = (((0,), (0,)), ((), ()))


def dot(a, b, dims):
    return lax.dot_general(a, b, dims, preferred_element_type=jnp.float32)


def choose(flag, a, b):
    return lax.select(flag, a, b)


def step_kernel(
    sizes,
    table,
    token_count,
    own_ref,
    q_ref,
    k_ref,
    v_ref,
    w_ref,
    og_ref,
    attn_ref,
    grad_ref,
    slab,
    queries,
    heads_grad,
    scaled_grad,
    exps,
    slopes,
    numer,
    denom,
    hg_send,
    hg_recv,
    stat_send,
    stat_recv,
    rows,
    num_send,
    num_recv,
    heads,
    part,
    own_sum,
    ring_send,
    ring_recv,
    ag_send_sem,
    ag_recv_sem,
    q_send_sem,
    q_recv_sem,
    g_send_sem,
    g_recv_sem,
    h_send_sem,
    h_recv_sem,
    s_send_sem,
    s_recv_sem,
    n_send_sem,
    n_recv_sem,
    a_send_sem,
    a_recv_sem,
    rs_send_sem,
    rs_recv_sem,
):
    Z, X, M, lag = sizes
    H = Z // 2
    tokens = q_ref.shape[0]
    group = q_ref.shape[1] // HD
    req, m = lax.axis_index("req"), lax.axis_index("mp")
    z, x = req // X, req % X
    right = {"req": ((z + 1) % Z) * X + x}
    left = {"req": ((z + Z - 1) % Z) * X + x}
    toward = (right, left)

    def x_peer(i):
        return {"req": z * X + (x + i) % X}

    def m_peer(i):
        return {"mp": (m + i) % M}

    def remote(src, dst, send_sem, recv_sem, device):
        return pltpu.make_async_remote_copy(
            src_ref=src,
            dst_ref=dst,
            send_sem=send_sem,
            recv_sem=recv_sem,
            device_id=device,
            device_id_type=pl.DeviceIdType.MESH,
        )

    def gather_hop(way, kind, hop):
        lane = way
        if way == LEFT and kind == VALUE:
            lane = 1 - hop // H
        return remote(
            slab.at[way, hop - 1, kind],
            slab.at[lane, hop, kind],
            ag_send_sem.at[way, hop, kind],
            ag_recv_sem.at[way, hop, kind],
            toward[way],
        )

    def last_hop(way, kind):
        return H if way == kind else H - 1

    def q_copy(i):
        return remote(
            q_ref, queries.at[x], q_send_sem.at[i], q_recv_sem.at[i], x_peer(i)
        )

    def g_copy(i):
        return remote(
            heads_grad.at[x], heads_grad.at[x], g_send_sem.at[i], g_recv_sem.at[i], x_peer(i)
        )

    def h_copy(i):
        return remote(
            hg_send.at[i], hg_recv.at[i], h_send_sem.at[i], h_recv_sem.at[i], m_peer(i)
        )

    def s_copy(i):
        return remote(stat_send, stat_recv.at[i], s_send_sem.at[i], s_recv_sem.at[i], x_peer(i))

    def n_copy(i):
        return remote(
            num_send.at[(x + i) % X], num_recv.at[i], n_send_sem.at[i], n_recv_sem.at[i], x_peer(i)
        )

    def a_copy(i):
        return remote(heads.at[m], heads.at[m], a_send_sem.at[i], a_recv_sem.at[i], m_peer(i))

    def ring_hop(way, kind, dist):
        return remote(
            ring_send.at[way, dist, kind],
            ring_recv.at[way, dist - 1, kind],
            rs_send_sem.at[way, dist, kind],
            rs_recv_sem.at[way, dist, kind],
            toward[way],
        )

    barrier = pltpu.get_barrier_semaphore()
    partners = [right, left] + [x_peer(i) for i in range(1, X)] + [m_peer(i) for i in range(1, M)]
    for partner in partners:
        pl.semaphore_signal(
            barrier, inc=1, device_id=partner, device_id_type=pl.DeviceIdType.MESH
        )
    own = own_ref[...]
    slab[RIGHT, 0] = own
    slab[LEFT, 0] = own
    slab[LEFT, H] = own
    queries[x] = q_ref[...]
    pl.semaphore_wait(barrier, len(partners))

    for kind in (KEY, VALUE):
        for way in (RIGHT, LEFT):
            gather_hop(way, kind, 1).start()
    for i in range(1, X):
        q_copy(i).start()

    def share(i, carry):
        target = (m + i) % M
        band = pl.ds(pl.multiple_of(target * (group * HD), group * HD), group * HD)
        hg_send[i] = dot(w_ref[band, :], og_ref[...], NT).astype(jnp.bfloat16)
        return carry

    for i in range(1, M):
        share(i, 0)
        h_copy(i).start()
    share(0, 0)

    numer[...] = jnp.zeros_like(numer)
    denom[...] = jnp.zeros_like(denom)
    key_pos = lax.broadcasted_iota(jnp.int32, (tokens, tokens), 0)
    query_pos = lax.broadcasted_iota(jnp.int32, (tokens, tokens), 1)
    causal = key_pos <= query_pos
    for g in range(group):
        lanes = slice(g * HD, (g + 1) * HD)
        score = dot(k_ref[...], q_ref[:, lanes], NT)
        exp = jnp.exp(softcap * jnp.tanh(score * (qscale / softcap)))
        exp = jnp.where(causal, exp, 0.0)
        denom[x, g : g + 1, :] = jnp.sum(exp, axis=0, keepdims=True)
        numer[x, lanes, :] = dot(v_ref[...], exp.astype(jnp.bfloat16), TN)

    def pick(code, way, step, kind):
        return choose(
            code == 2, slab[way, step, kind, BLOCK:, :], slab[way, step, kind, :BLOCK, :]
        )

    def forward(step):
        def request(r, carry):
            code_a, code_b = table[0, r, step], table[1, r, step]
            keys = jnp.concatenate(
                [pick(code_a, 0, step, KEY), pick(code_b, 1, step, KEY)], axis=0
            )
            val_a, val_b = pick(code_a, 0, step, VALUE), pick(code_b, 1, step, VALUE)
            zero = jnp.zeros_like(val_a)
            vals = jnp.concatenate(
                [choose(code_a > 0, val_a, zero), choose(code_b > 0, val_b, zero)], axis=0
            )
            for g in range(group):
                lanes = slice(g * HD, (g + 1) * HD)
                tanh = jnp.tanh(dot(keys, queries[r, :, lanes], NT) * (qscale / softcap))
                exp = jnp.exp(softcap * tanh)
                half = exp.astype(jnp.bfloat16)
                exps[step - 1, r, g] = half
                slopes[step - 1, r, g] = (exp * (1.0 - tanh * tanh)).astype(jnp.bfloat16)
                sum_a = jnp.sum(exp[:BLOCK], axis=0, keepdims=True)
                sum_b = jnp.sum(exp[BLOCK:], axis=0, keepdims=True)
                none = jnp.zeros_like(sum_a)
                denom[r, g : g + 1, :] += choose(code_a > 0, sum_a, none) + choose(
                    code_b > 0, sum_b, none
                )
                numer[r, lanes, :] += dot(vals, half, TN)
            return carry

        lax.fori_loop(0, X, request, 0)

    live = lax.broadcasted_iota(jnp.int32, (group * HD, tokens), 1) < token_count[0]

    def gather_step(step, carry):
        for kind in (KEY, VALUE):
            for way in (RIGHT, LEFT):
                last = last_hop(way, kind)

                @pl.when(step <= last)
                def _():
                    gather_hop(way, kind, step).wait_recv()

                @pl.when(step < last)
                def _():
                    gather_hop(way, kind, step + 1).start()

        @pl.when(step == lag + 1)
        def _():
            for i in range(1, X):
                q_copy(i).wait_recv()

        @pl.when(step > lag)
        def _():
            forward(step - lag)

        @pl.when(step == min(lag + 3, H))
        def _():
            total = hg_send[0].astype(jnp.float32)
            for i in range(1, M):
                h_copy(i).wait_recv()
                total += hg_recv[i].astype(jnp.float32)
            heads_grad[x] = jnp.where(live, total, 0.0).astype(jnp.bfloat16)
            for i in range(1, X):
                g_copy(i).start()

        return carry

    lax.fori_loop(1, H + 1, gather_step, 0)

    def late(step, carry):
        forward(step)
        return carry

    lax.fori_loop(H + 1 - lag, H + 1, late, 0)

    for i in range(1, X):
        g_copy(i).wait_recv()
    for r in range(X):
        for g in range(group):
            lanes = slice(g * HD, (g + 1) * HD)
            row = (r * group + g) * 2
            stat_send[row : row + 1, :] = denom[r, g : g + 1, :]
            stat_send[row + 1 : row + 2, :] = jnp.sum(
                heads_grad[r, lanes, :].astype(jnp.float32) * numer[r, lanes, :],
                axis=0,
                keepdims=True,
            )
    for i in range(1, X):
        s_copy(i).start()
    num_send[...] = numer[...].astype(jnp.bfloat16)
    for i in range(1, X):
        n_copy(i).start()
    ring_recv[RIGHT, H - 1, VALUE] = jnp.zeros_like(ring_recv[RIGHT, H - 1, VALUE])
    ring_recv[LEFT, H - 1, KEY] = jnp.zeros_like(ring_recv[LEFT, H - 1, KEY])
    stats = stat_send[...]
    for i in range(1, X):
        s_copy(i).wait_recv()
        stats += stat_recv[i]
    for r in range(X):
        for g in range(group):
            lanes = slice(g * HD, (g + 1) * HD)
            row = (r * group + g) * 2
            inverse = 1.0 / stats[row : row + 1, :]
            rows[r, 2 * g : 2 * g + 1, :] = inverse
            rows[r, 2 * g + 1 : 2 * g + 2, :] = inverse * stats[row + 1 : row + 2, :]
            scaled_grad[r, lanes, :] = (
                heads_grad[r, lanes, :].astype(jnp.float32) * inverse
            ).astype(jnp.bfloat16)

    def backward(dist):
        part[...] = jnp.zeros_like(part)

        def request(r, carry):
            code_a, code_b = table[0, r, dist], table[1, r, dist]
            vals = jnp.concatenate(
                [pick(code_a, 0, dist, VALUE), pick(code_b, 1, dist, VALUE)], axis=0
            )
            key_grad = jnp.zeros((2 * BLOCK, HD), jnp.float32)
            value_grad = jnp.zeros((2 * BLOCK, HD), jnp.float32)
            for g in range(group):
                lanes = slice(g * HD, (g + 1) * HD)
                inverse = rows[r, 2 * g : 2 * g + 1, :]
                delta = rows[r, 2 * g + 1 : 2 * g + 2, :]
                dprob = dot(vals, heads_grad[r, lanes, :], NN)
                slope = slopes[dist - 1, r, g].astype(jnp.float32)
                dscore = slope * ((dprob - delta) * (inverse * qscale))
                key_grad += dot(dscore.astype(jnp.bfloat16), queries[r, :, lanes], NN)
                value_grad += dot(exps[dist - 1, r, g], scaled_grad[r, lanes, :], NT)
            none = jnp.zeros((BLOCK, HD), jnp.float32)
            for side, code in enumerate((code_a, code_b)):
                span = slice(side * BLOCK, (side + 1) * BLOCK)
                for block in range(2):
                    place = slice(block * BLOCK, (block + 1) * BLOCK)
                    hit = code == block + 1
                    part[side, KEY, place, :] += choose(hit, key_grad[span], none)
                    part[side, VALUE, place, :] += choose(hit, value_grad[span], none)
            return carry

        lax.fori_loop(0, X, request, 0)

    def scatter_step(index, carry):
        dist = H - index
        backward(dist)

        @pl.when(index == 0)
        def _():
            own_sum[...] = part[1]
            ring_send[RIGHT, H, KEY] = part[0, KEY].astype(jnp.bfloat16)
            ring_send[LEFT, H, VALUE] = part[0, VALUE].astype(jnp.bfloat16)
            ring_hop(RIGHT, KEY, H).start()
            ring_hop(LEFT, VALUE, H).start()

        @pl.when(index > 0)
        def _():
            for kind in (KEY, VALUE):
                for way in (RIGHT, LEFT):

                    @pl.when(dist + 1 <= last_hop(way, kind))
                    def _():
                        ring_hop(way, kind, dist + 1).wait_recv()

                    ring_send[way, dist, kind] = (
                        part[1 - way, kind] + ring_recv[way, dist, kind].astype(jnp.float32)
                    ).astype(jnp.bfloat16)
                    ring_hop(way, kind, dist).start()

        @pl.when(index == min(3, H - 1))
        def _():
            total = numer[x]
            for i in range(1, X):
                n_copy(i).wait_recv()
                total += num_recv[i].astype(jnp.float32)
            out = jnp.concatenate(
                [total[g * HD : (g + 1) * HD] * rows[x, 2 * g : 2 * g + 1, :] for g in range(group)],
                axis=0,
            )
            heads[m] = jnp.where(live, out, 0.0).T.astype(jnp.bfloat16)
            for i in range(1, M):
                a_copy(i).start()

        return carry

    lax.fori_loop(0, H, scatter_step, 0)

    for i in range(1, M):
        a_copy(i).wait_recv()
    attn_ref[...] = dot(heads[0], w_ref[: group * HD, :], NN)

    def project(j, carry):
        band = pl.ds(pl.multiple_of(j * (group * HD), group * HD), group * HD)
        attn_ref[...] += dot(heads[j], w_ref[band, :], NN)
        return carry

    lax.fori_loop(1, M, project, 0)

    for kind in (KEY, VALUE):
        total = own_sum[kind]
        for way in (RIGHT, LEFT):
            ring_hop(way, kind, 1).wait_recv()
            total += ring_recv[way, 0, kind].astype(jnp.float32)
        grad_ref[kind] = total

    for kind in (KEY, VALUE):
        for way in (RIGHT, LEFT):
            for hop in range(1, last_hop(way, kind) + 1):
                gather_hop(way, kind, hop).wait_send()
                ring_hop(way, kind, hop).wait_send()
    for i in range(1, X):
        q_copy(i).wait_send()
        g_copy(i).wait_send()
        s_copy(i).wait_send()
        n_copy(i).wait_send()
    for i in range(1, M):
        h_copy(i).wait_send()
        a_copy(i).wait_send()


def local(
    Z,
    X,
    queries,
    keys,
    values,
    out_weight,
    out_grad,
    bank,
    moment_one,
    moment_two,
    block_list,
    block_count,
    token_count,
):
    M = lax.axis_size("mp")
    H = Z // 2
    lag = 2 if H > 3 else 1
    req = lax.axis_index("req")
    z, x = req // X, req % X
    tokens, heads_width = queries.shape
    group = heads_width // HD
    width = out_weight.shape[1]
    blk_dev = bank.shape[0] // BLOCK

    lists = lax.dynamic_slice_in_dim(block_list, z * X, X, 0)
    counts = lax.dynamic_slice_in_dim(block_count, z * X, X, 0)
    steps = jnp.arange(H + 1, dtype=jnp.int32)
    behind = ((z - steps) % Z) * X + x
    ahead = jnp.where(steps == H, z, (z + steps) % Z) * X + x
    owners = jnp.stack([behind, ahead])
    used = lax.broadcasted_iota(jnp.int32, lists.shape, 1) < counts[:, None]
    hit = used[None, :, None, :] & (lists[None, :, None, :] // blk_dev == owners[:, None, :, None])
    table = jnp.sum(jnp.where(hit, 1 + lists[None, :, None, :] % blk_dev, 0), axis=-1)

    own = jnp.transpose(bank.astype(jnp.bfloat16), (1, 0, 2))
    bf16, f32 = jnp.bfloat16, jnp.float32
    rows_local = bank.shape[0]
    vmem = pltpu.VMEM
    dma = pltpu.SemaphoreType.DMA
    smem_spec = pl.BlockSpec(memory_space=pltpu.SMEM)
    vmem_spec = pl.BlockSpec(memory_space=pltpu.VMEM)
    attn_out, grad = pl.pallas_call(
        functools.partial(step_kernel, (Z, X, M, lag)),
        out_shape=(
            jax.ShapeDtypeStruct((tokens, width), f32),
            jax.ShapeDtypeStruct((2, rows_local, HD), f32),
        ),
        in_specs=[smem_spec, smem_spec] + [vmem_spec] * 6,
        out_specs=(vmem_spec, vmem_spec),
        scratch_shapes=[
            vmem((2, H + 1, 2, rows_local, HD), bf16),
            vmem((X, tokens, heads_width), bf16),
            vmem((X, heads_width, tokens), bf16),
            vmem((X, heads_width, tokens), bf16),
            vmem((H, X, group, 2 * BLOCK, tokens), bf16),
            vmem((H, X, group, 2 * BLOCK, tokens), bf16),
            vmem((X, heads_width, tokens), f32),
            vmem((X, group, tokens), f32),
            vmem((M, heads_width, tokens), bf16),
            vmem((M, heads_width, tokens), bf16),
            vmem((2 * X * group, tokens), f32),
            vmem((X, 2 * X * group, tokens), f32),
            vmem((X, 2 * group, tokens), f32),
            vmem((X, heads_width, tokens), bf16),
            vmem((X, heads_width, tokens), bf16),
            vmem((M, tokens, heads_width), bf16),
            vmem((2, 2, rows_local, HD), f32),
            vmem((2, rows_local, HD), f32),
            vmem((2, H + 1, 2, rows_local, HD), bf16),
            vmem((2, H + 1, 2, rows_local, HD), bf16),
            dma((2, H + 1, 2)),
            dma((2, H + 1, 2)),
            dma((X,)),
            dma((X,)),
            dma((X,)),
            dma((X,)),
            dma((M,)),
            dma((M,)),
            dma((X,)),
            dma((X,)),
            dma((X,)),
            dma((X,)),
            dma((M,)),
            dma((M,)),
            dma((2, H + 1, 2)),
            dma((2, H + 1, 2)),
        ],
        compiler_params=pltpu.CompilerParams(
            collective_id=0, has_side_effects=True, vmem_limit_bytes=56 << 20
        ),
    )(table, token_count, own, queries, keys, values, out_weight, out_grad)

    block_grad = jnp.transpose(grad, (1, 0, 2))
    moment_next = beta_one * moment_one + (1.0 - beta_one) * block_grad
    second_next = beta_two * moment_two + (1.0 - beta_two) * block_grad * block_grad
    bank_next = bank - learn_rate * (moment_next / bias_one) / (
        jnp.sqrt(second_next / bias_two) + adam_eps
    )
    return (attn_out, bank_next, moment_next, second_next)


def solution(mesh):
    reqs = mesh.shape["req"]
    X = 4 if reqs >= 64 else 2
    return jax.shard_map(
        functools.partial(local, reqs // X, X),
        mesh=mesh,
        in_specs=(
            P("req", "mp"),
            P("req", "mp"),
            P("req", "mp"),
            P(None, "mp"),
            P("req", "mp"),
            P("req", None, "mp"),
            P("req", None, "mp"),
            P("req", None, "mp"),
            P(),
            P(),
            P("req"),
        ),
        out_specs=(
            P("req", "mp"),
            P("req", None, "mp"),
            P("req", None, "mp"),
            P("req", None, "mp"),
        ),
        check_vma=False,
    )
```

```python
import functools

import jax
import jax.numpy as jnp
from jax import lax
from jax.experimental import pallas as pl
from jax.experimental.pallas import tpu as pltpu
from jax.sharding import PartitionSpec as P

HD = 128
BLOCK = 128
KEY, VALUE = 0, 1
RIGHT, LEFT = 0, 1

softcap = 50.0
qscale = 1.0 / 12.0
beta_one = 0.9
beta_two = 0.999
learn_rate = 0.3
adam_eps = 1e-08
bias_one = 1.0 - 0.9**10
bias_two = 1.0 - 0.999**10

NN = (((1,), (0,)), ((), ()))
NT = (((1,), (1,)), ((), ()))
TN = (((0,), (0,)), ((), ()))


def dot(a, b, dims):
    return lax.dot_general(a, b, dims, preferred_element_type=jnp.float32)


def choose(flag, a, b):
    return lax.select(flag, a, b)


def step_kernel(
    sizes,
    table,
    token_count,
    bank_ref,
    q_ref,
    k_ref,
    v_ref,
    w_ref,
    og_ref,
    attn_ref,
    grad_ref,
    slab,
    queries,
    heads_grad,
    scaled_grad,
    exps,
    slopes,
    numer,
    denom,
    hg_send,
    hg_recv,
    stat_send,
    stat_recv,
    rows,
    num_send,
    num_recv,
    heads,
    part,
    own_sum,
    ring_send,
    ring_recv,
    ag_send_sem,
    ag_recv_sem,
    q_send_sem,
    q_recv_sem,
    g_send_sem,
    g_recv_sem,
    h_send_sem,
    h_recv_sem,
    s_send_sem,
    s_recv_sem,
    n_send_sem,
    n_recv_sem,
    a_send_sem,
    a_recv_sem,
    rs_send_sem,
    rs_recv_sem,
):
    Z, X, M = sizes
    H = Z // 2
    tokens = q_ref.shape[0]
    group = q_ref.shape[1] // HD
    req, m = lax.axis_index("req"), lax.axis_index("mp")
    z, x = req // X, req % X
    right = {"req": ((z + 1) % Z) * X + x}
    left = {"req": ((z + Z - 1) % Z) * X + x}
    toward = (right, left)

    def x_peer(i):
        return {"req": z * X + (x + i) % X}

    def m_peer(i):
        return {"mp": (m + i) % M}

    def remote(src, dst, send_sem, recv_sem, device):
        return pltpu.make_async_remote_copy(
            src_ref=src,
            dst_ref=dst,
            send_sem=send_sem,
            recv_sem=recv_sem,
            device_id=device,
            device_id_type=pl.DeviceIdType.MESH,
        )

    def gather_hop(way, kind, half, hop):
        lane = way
        if way == LEFT and kind == VALUE:
            lane = 1 - hop // H
        span = pl.ds(half * BLOCK, BLOCK)
        return remote(
            slab.at[way, hop - 1, kind, span],
            slab.at[lane, hop, kind, span],
            ag_send_sem.at[way, hop, 2 * kind + half],
            ag_recv_sem.at[way, hop, 2 * kind + half],
            toward[way],
        )

    def last_hop(way, kind):
        return H if way == kind else H - 1

    def q_copy(i):
        return remote(
            q_ref, queries.at[x], q_send_sem.at[i], q_recv_sem.at[i], x_peer(i)
        )

    def g_copy(i):
        return remote(
            heads_grad.at[x], heads_grad.at[x], g_send_sem.at[i], g_recv_sem.at[i], x_peer(i)
        )

    def h_copy(i):
        return remote(
            hg_send.at[i], hg_recv.at[i], h_send_sem.at[i], h_recv_sem.at[i], m_peer(i)
        )

    def s_copy(i):
        return remote(stat_send, stat_recv.at[i], s_send_sem.at[i], s_recv_sem.at[i], x_peer(i))

    def n_copy(i):
        return remote(
            num_send.at[(x + i) % X], num_recv.at[i], n_send_sem.at[i], n_recv_sem.at[i], x_peer(i)
        )

    def a_copy(i):
        return remote(heads.at[m], heads.at[m], a_send_sem.at[i], a_recv_sem.at[i], m_peer(i))

    def ring_hop(way, kind, half, dist):
        span = pl.ds(half * BLOCK, BLOCK)
        return remote(
            ring_send.at[way, dist, kind, span],
            ring_recv.at[way, dist - 1, kind, span],
            rs_send_sem.at[way, dist, 2 * kind + half],
            rs_recv_sem.at[way, dist, 2 * kind + half],
            toward[way],
        )

    barrier = pltpu.get_barrier_semaphore()
    partners = [right, left] + [x_peer(i) for i in range(1, X)] + [m_peer(i) for i in range(1, M)]
    for partner in partners:
        pl.semaphore_signal(
            barrier, inc=1, device_id=partner, device_id_type=pl.DeviceIdType.MESH
        )
    for kind in (KEY, VALUE):
        own = bank_ref[pl.ds(kind, 2 * BLOCK, stride=2), :].astype(jnp.bfloat16)
        slab[RIGHT, 0, kind] = own
        slab[LEFT, 0, kind] = own
        slab[LEFT, H, kind] = own
    queries[x] = q_ref[...]
    pl.semaphore_wait(barrier, len(partners))

    near = [i for i in range(1, X) if i in (1, X - 1)]
    far = [i for i in range(1, X) if i not in near]
    order = [0] + near + far
    for kind in (KEY, VALUE):
        for half in range(2):
            for way in (RIGHT, LEFT):
                gather_hop(way, kind, half, 1).start()
    for i in order[1:]:
        q_copy(i).start()

    og = og_ref[...].T

    def share(i):
        target = (m + i) % M
        band = pl.ds(pl.multiple_of(target * (group * HD), group * HD), group * HD)
        hg_send[i] = dot(og, w_ref[:, band], NN).astype(jnp.bfloat16)

    for i in range(1, M):
        share(i)
        h_copy(i).start()
    share(0)

    numer[...] = jnp.zeros_like(numer)
    denom[...] = jnp.zeros_like(denom)
    key_pos = lax.broadcasted_iota(jnp.int32, (tokens, tokens), 0)
    query_pos = lax.broadcasted_iota(jnp.int32, (tokens, tokens), 1)
    causal = key_pos <= query_pos
    for g in range(group):
        lanes = slice(g * HD, (g + 1) * HD)
        score = dot(k_ref[...], q_ref[:, lanes], NT)
        exp = jnp.exp(softcap * jnp.tanh(score * (qscale / softcap)))
        exp = jnp.where(causal, exp, 0.0)
        denom[x, g : g + 1, :] = jnp.sum(exp, axis=0, keepdims=True)
        numer[x, lanes, :] = dot(v_ref[...], exp.astype(jnp.bfloat16), TN)

    def pick(code, way, step, kind):
        return choose(
            code == 2, slab[way, step, kind, BLOCK:, :], slab[way, step, kind, :BLOCK, :]
        )

    def forward(step, offsets):
        for offset in offsets:
            r = (x + offset) % X
            code_a, code_b = table[0, r, step], table[1, r, step]
            keys = jnp.concatenate(
                [pick(code_a, 0, step, KEY), pick(code_b, 1, step, KEY)], axis=0
            )
            val_a, val_b = pick(code_a, 0, step, VALUE), pick(code_b, 1, step, VALUE)
            zero = jnp.zeros_like(val_a)
            vals = jnp.concatenate(
                [choose(code_a > 0, val_a, zero), choose(code_b > 0, val_b, zero)], axis=0
            )
            halves = []
            for g in range(group):
                lanes = slice(g * HD, (g + 1) * HD)
                tanh = jnp.tanh(dot(keys, queries[r, :, lanes], NT) * (qscale / softcap))
                exp = jnp.exp(softcap * tanh)
                half = exp.astype(jnp.bfloat16)
                halves.append(half)
                exps[step - 1, r, g] = half
                slopes[step - 1, r, g] = (exp * (1.0 - tanh * tanh)).astype(jnp.bfloat16)
                sum_a = jnp.sum(exp[:BLOCK], axis=0, keepdims=True)
                sum_b = jnp.sum(exp[BLOCK:], axis=0, keepdims=True)
                none = jnp.zeros_like(sum_a)
                denom[r, g : g + 1, :] += choose(code_a > 0, sum_a, none) + choose(
                    code_b > 0, sum_b, none
                )
            mixed = dot(vals, jnp.concatenate(halves, axis=1), TN)
            for g in range(group):
                numer[r, g * HD : (g + 1) * HD, :] += mixed[:, g * tokens : (g + 1) * tokens]

    live = lax.broadcasted_iota(jnp.int32, (group * HD, tokens), 1) < token_count[0]
    early, late = order[: X // 2], order[X // 2 :]

    def pass_on(step, kind):
        for half in range(2):
            for way in (RIGHT, LEFT):
                last = last_hop(way, kind)

                @pl.when(step <= last)
                def _():
                    gather_hop(way, kind, half, step).wait_recv()

                @pl.when(step < last)
                def _():
                    gather_hop(way, kind, half, step + 1).start()

    def gather_step(step, carry):
        @pl.when(step <= H)
        def _():
            pass_on(step, KEY)

        @pl.when(step == 2)
        def _():
            for i in late:
                q_copy(X - i).wait_recv()

        @pl.when(step > 1)
        def _():
            forward(step - 1, late)

        @pl.when(step <= H)
        def _():
            pass_on(step, VALUE)

        @pl.when(step == 1)
        def _():
            for i in early[1:]:
                q_copy(X - i).wait_recv()

        @pl.when(step <= H)
        def _():
            forward(step, early)

        @pl.when(step == min(6, H))
        def _():
            total = hg_send[0].astype(jnp.float32)
            for i in range(1, M):
                h_copy(i).wait_recv()
                total += hg_recv[i].astype(jnp.float32)
            heads_grad[x] = jnp.where(live, total.T, 0.0).astype(jnp.bfloat16)
            for i in order[1:]:
                g_copy(i).start()

        return carry

    lax.fori_loop(1, H + 2, gather_step, 0)

    for i in range(1, X):
        g_copy(i).wait_recv()
    for r in range(X):
        for g in range(group):
            lanes = slice(g * HD, (g + 1) * HD)
            row = (r * group + g) * 2
            stat_send[row : row + 1, :] = denom[r, g : g + 1, :]
            stat_send[row + 1 : row + 2, :] = jnp.sum(
                heads_grad[r, lanes, :].astype(jnp.float32) * numer[r, lanes, :],
                axis=0,
                keepdims=True,
            )
    for i in order[1:]:
        s_copy(i).start()
    num_send[...] = numer[...].astype(jnp.bfloat16)
    for i in order[1:]:
        n_copy(i).start()
    ring_recv[RIGHT, H - 1, VALUE] = jnp.zeros_like(ring_recv[RIGHT, H - 1, VALUE])
    ring_recv[LEFT, H - 1, KEY] = jnp.zeros_like(ring_recv[LEFT, H - 1, KEY])
    stats = stat_send[...]
    for i in range(1, X):
        s_copy(i).wait_recv()
        stats += stat_recv[i]
    for r in range(X):
        for g in range(group):
            lanes = slice(g * HD, (g + 1) * HD)
            row = (r * group + g) * 2
            inverse = 1.0 / stats[row : row + 1, :]
            rows[r, 2 * g : 2 * g + 1, :] = inverse
            rows[r, 2 * g + 1 : 2 * g + 2, :] = inverse * stats[row + 1 : row + 2, :]
            scaled_grad[r, lanes, :] = (
                heads_grad[r, lanes, :].astype(jnp.float32) * inverse
            ).astype(jnp.bfloat16)

    def backward(dist, requests, first):
        slot = dist % 2
        found = []
        for r in requests:
            code_a, code_b = table[0, r, dist], table[1, r, dist]
            vals = jnp.concatenate(
                [pick(code_a, 0, dist, VALUE), pick(code_b, 1, dist, VALUE)], axis=0
            )
            key_grad = jnp.zeros((2 * BLOCK, HD), jnp.float32)
            value_grad = jnp.zeros((2 * BLOCK, HD), jnp.float32)
            for g in range(group):
                lanes = slice(g * HD, (g + 1) * HD)
                inverse = rows[r, 2 * g : 2 * g + 1, :]
                delta = rows[r, 2 * g + 1 : 2 * g + 2, :]
                dprob = dot(vals, heads_grad[r, lanes, :], NN)
                slope = slopes[dist - 1, r, g].astype(jnp.float32)
                dscore = slope * ((dprob - delta) * (inverse * qscale))
                key_grad += dot(dscore.astype(jnp.bfloat16), queries[r, :, lanes], NN)
                value_grad += dot(exps[dist - 1, r, g], scaled_grad[r, lanes, :], NT)
            found.append(((code_a, code_b), (key_grad, value_grad)))
        none = jnp.zeros((BLOCK, HD), jnp.float32)
        for side in range(2):
            span = slice(side * BLOCK, (side + 1) * BLOCK)
            for kind in (KEY, VALUE):
                for block in range(2):
                    place = slice(block * BLOCK, (block + 1) * BLOCK)
                    total = none if first else part[slot, side, kind, place, :]
                    for codes, grads in found:
                        total += choose(codes[side] == block + 1, grads[kind][span], none)
                    part[slot, side, kind, place, :] = total

    def hand_over(dist, kind):
        slot = dist % 2
        for half in range(2):
            span = slice(half * BLOCK, (half + 1) * BLOCK)
            for way in (RIGHT, LEFT):
                last = last_hop(way, kind)
                side = 1 - way

                @pl.when(dist == H)
                def _():
                    if way == kind:
                        ring_send[way, H, kind, span, :] = part[slot, 0, kind, span, :].astype(
                            jnp.bfloat16
                        )
                        ring_hop(way, kind, half, H).start()

                @pl.when(dist < H)
                def _():
                    @pl.when(dist < last)
                    def _():
                        ring_hop(way, kind, half, dist + 1).wait_recv()

                    ring_send[way, dist, kind, span, :] = (
                        part[slot, side, kind, span, :]
                        + ring_recv[way, dist, kind, span, :].astype(jnp.float32)
                    ).astype(jnp.bfloat16)
                    ring_hop(way, kind, half, dist).start()

    def scatter_step(index, carry):
        dist = H + 1 - index

        @pl.when(dist <= H)
        def _():
            hand_over(dist, KEY)

        @pl.when(dist > 1)
        def _():
            backward(dist - 1, range(X // 2), True)

        @pl.when(dist <= H)
        def _():
            hand_over(dist, VALUE)

        @pl.when(dist > 1)
        def _():
            backward(dist - 1, range(X // 2, X), False)

        @pl.when(index == 0)
        def _():
            own_sum[...] = part[H % 2, 1]

        @pl.when(index == min(4, H))
        def _():
            total = numer[x]
            for i in range(1, X):
                n_copy(i).wait_recv()
                total += num_recv[i].astype(jnp.float32)
            out = jnp.concatenate(
                [total[g * HD : (g + 1) * HD] * rows[x, 2 * g : 2 * g + 1, :] for g in range(group)],
                axis=0,
            )
            heads[m] = jnp.where(live, out, 0.0).astype(jnp.bfloat16)
            for i in range(1, M):
                a_copy(i).start()

        return carry

    lax.fori_loop(0, H + 1, scatter_step, 0)

    for i in range(1, M):
        a_copy(i).wait_recv()
    depth = group * HD
    total = dot(w_ref[:, :depth], heads[0], NN)
    for j in range(1, M):
        total += dot(w_ref[:, j * depth : (j + 1) * depth], heads[j], NN)
    attn_ref[...] = total

    for kind in (KEY, VALUE):
        for half in range(2):
            for way in (RIGHT, LEFT):
                ring_hop(way, kind, half, 1).wait_recv()
        total = own_sum[kind]
        for way in (RIGHT, LEFT):
            total += ring_recv[way, 0, kind].astype(jnp.float32)
        grad_ref[pl.ds(kind, 2 * BLOCK, stride=2), :] = total

    for kind in (KEY, VALUE):
        for way in (RIGHT, LEFT):
            for hop in range(1, last_hop(way, kind) + 1):
                for half in range(2):
                    gather_hop(way, kind, half, hop).wait_send()
                    ring_hop(way, kind, half, hop).wait_send()
    for i in range(1, X):
        q_copy(i).wait_send()
        g_copy(i).wait_send()
        s_copy(i).wait_send()
        n_copy(i).wait_send()
    for i in range(1, M):
        h_copy(i).wait_send()
        a_copy(i).wait_send()


def local(
    Z,
    X,
    queries,
    keys,
    values,
    out_weight,
    out_grad,
    bank,
    moment_one,
    moment_two,
    block_list,
    block_count,
    token_count,
):
    M = lax.axis_size("mp")
    H = Z // 2
    req = lax.axis_index("req")
    z, x = req // X, req % X
    tokens, heads_width = queries.shape
    group = heads_width // HD
    width = out_weight.shape[1]
    blk_dev = bank.shape[0] // BLOCK

    lists = lax.dynamic_slice_in_dim(block_list, z * X, X, 0)
    counts = lax.dynamic_slice_in_dim(block_count, z * X, X, 0)
    steps = jnp.arange(H + 1, dtype=jnp.int32)
    behind = ((z - steps) % Z) * X + x
    ahead = jnp.where(steps == H, z, (z + steps) % Z) * X + x
    owners = jnp.stack([behind, ahead])
    used = lax.broadcasted_iota(jnp.int32, lists.shape, 1) < counts[:, None]
    hit = used[None, :, None, :] & (lists[None, :, None, :] // blk_dev == owners[:, None, :, None])
    table = jnp.sum(jnp.where(hit, 1 + lists[None, :, None, :] % blk_dev, 0), axis=-1)

    flat = (2 * bank.shape[0], HD)
    bf16, f32 = jnp.bfloat16, jnp.float32
    rows_local = bank.shape[0]
    vmem = pltpu.VMEM
    dma = pltpu.SemaphoreType.DMA
    smem_spec = pl.BlockSpec(memory_space=pltpu.SMEM)
    vmem_spec = pl.BlockSpec(memory_space=pltpu.VMEM)
    attn_out, grad = pl.pallas_call(
        functools.partial(step_kernel, (Z, X, M)),
        out_shape=(
            jax.ShapeDtypeStruct((width, tokens), f32),
            jax.ShapeDtypeStruct(flat, f32),
        ),
        in_specs=[smem_spec, smem_spec] + [vmem_spec] * 6,
        out_specs=(vmem_spec, vmem_spec),
        scratch_shapes=[
            vmem((2, H + 1, 2, rows_local, HD), bf16),
            vmem((X, tokens, heads_width), bf16),
            vmem((X, heads_width, tokens), bf16),
            vmem((X, heads_width, tokens), bf16),
            vmem((H, X, group, 2 * BLOCK, tokens), bf16),
            vmem((H, X, group, 2 * BLOCK, tokens), bf16),
            vmem((X, heads_width, tokens), f32),
            vmem((X, group, tokens), f32),
            vmem((M, tokens, heads_width), bf16),
            vmem((M, tokens, heads_width), bf16),
            vmem((2 * X * group, tokens), f32),
            vmem((X, 2 * X * group, tokens), f32),
            vmem((X, 2 * group, tokens), f32),
            vmem((X, heads_width, tokens), bf16),
            vmem((X, heads_width, tokens), bf16),
            vmem((M, heads_width, tokens), bf16),
            vmem((2, 2, 2, rows_local, HD), f32),
            vmem((2, rows_local, HD), f32),
            vmem((2, H + 1, 2, rows_local, HD), bf16),
            vmem((2, H + 1, 2, rows_local, HD), bf16),
            dma((2, H + 1, 4)),
            dma((2, H + 1, 4)),
            dma((X,)),
            dma((X,)),
            dma((X,)),
            dma((X,)),
            dma((M,)),
            dma((M,)),
            dma((X,)),
            dma((X,)),
            dma((X,)),
            dma((X,)),
            dma((M,)),
            dma((M,)),
            dma((2, H + 1, 4)),
            dma((2, H + 1, 4)),
        ],
        compiler_params=pltpu.CompilerParams(
            collective_id=0, has_side_effects=True, vmem_limit_bytes=56 << 20
        ),
    )(
        table,
        token_count,
        bank.reshape(flat),
        queries,
        keys,
        values,
        out_weight.T,
        out_grad.T,
    )

    one, two = moment_one.reshape(flat), moment_two.reshape(flat)
    moment_next = beta_one * one + (1.0 - beta_one) * grad
    second_next = beta_two * two + (1.0 - beta_two) * grad * grad
    bank_next = bank.reshape(flat) - learn_rate * (moment_next / bias_one) / (
        jnp.sqrt(second_next / bias_two) + adam_eps
    )
    return (
        attn_out.T,
        bank_next.reshape(bank.shape),
        moment_next.reshape(bank.shape),
        second_next.reshape(bank.shape),
    )


def solution(mesh):
    reqs = mesh.shape["req"]
    X = 4 if reqs >= 64 else 2
    return jax.shard_map(
        functools.partial(local, reqs // X, X),
        mesh=mesh,
        in_specs=(
            P("req", "mp"),
            P("req", "mp"),
            P("req", "mp"),
            P(None, "mp"),
            P("req", "mp"),
            P("req", None, "mp"),
            P("req", None, "mp"),
            P("req", None, "mp"),
            P(),
            P(),
            P("req"),
        ),
        out_specs=(
            P("req", "mp"),
            P("req", None, "mp"),
            P("req", None, "mp"),
            P("req", None, "mp"),
        ),
        check_vma=False,
    )
```

```python
import functools

import jax
import jax.numpy as jnp
from jax import lax
from jax.experimental import pallas as pl
from jax.experimental.pallas import tpu as pltpu
from jax.sharding import PartitionSpec as P

HD = 128
BLOCK = 128
KEY, VALUE = 0, 1
RIGHT, LEFT = 0, 1
AHEAD = 64

softcap = 50.0
qscale = 1.0 / 12.0
beta_one = 0.9
beta_two = 0.999
learn_rate = 0.3
adam_eps = 1e-08
bias_one = 1.0 - 0.9**10
bias_two = 1.0 - 0.999**10

NN = (((1,), (0,)), ((), ()))
NT = (((1,), (1,)), ((), ()))
TN = (((0,), (0,)), ((), ()))


def dot(a, b, dims):
    return lax.dot_general(a, b, dims, preferred_element_type=jnp.float32)


def choose(flag, a, b):
    return lax.select(flag, a, b)


def step_kernel(
    sizes,
    block_count,
    token_count,
    lists_ref,
    bank_ref,
    q_ref,
    k_ref,
    v_ref,
    w_hbm,
    og_hbm,
    attn_hbm,
    grad_ref,
    w_ref,
    og_ref,
    attn_ref,
    codes,
    table,
    slab,
    queries,
    heads_grad,
    scaled_grad,
    exps,
    slopes,
    numer,
    denom,
    hg_send,
    hg_recv,
    stat_send,
    stat_recv,
    rows,
    num_send,
    num_recv,
    heads,
    part,
    own_sum,
    ring_send,
    ring_recv,
    ag_send_sem,
    ag_recv_sem,
    q_send_sem,
    q_recv_sem,
    g_send_sem,
    g_recv_sem,
    h_send_sem,
    h_recv_sem,
    s_send_sem,
    s_recv_sem,
    n_send_sem,
    n_recv_sem,
    a_send_sem,
    a_recv_sem,
    rs_recv_sem,
    local_sem,
):
    Z, X, M = sizes
    H = Z // 2
    tokens = q_ref.shape[0]
    group = q_ref.shape[1] // HD
    req, m = lax.axis_index("req"), lax.axis_index("mp")
    z, x = req // X, req % X
    right = {"req": ((z + 1) % Z) * X + x}
    left = {"req": ((z + Z - 1) % Z) * X + x}
    toward = (right, left)

    def x_peer(i):
        return {"req": z * X + (x + i) % X}

    def m_peer(i):
        return {"mp": (m + i) % M}

    def remote(src, dst, send_sem, recv_sem, device):
        return pltpu.make_async_remote_copy(
            src_ref=src,
            dst_ref=dst,
            send_sem=send_sem,
            recv_sem=recv_sem,
            device_id=device,
            device_id_type=pl.DeviceIdType.MESH,
        )

    def gather_hop(way, kind, half, hop):
        lane = way
        if way == LEFT and kind == VALUE:
            lane = 1 - hop // H
        span = pl.ds(half * BLOCK, BLOCK)
        return remote(
            slab.at[way, hop - 1, kind, span],
            slab.at[lane, hop, kind, span],
            ag_send_sem.at[way, hop, 2 * kind + half],
            ag_recv_sem.at[way, hop, 2 * kind + half],
            toward[way],
        )

    def last_hop(way, kind):
        return H if way == kind else H - 1

    def q_copy(i):
        return remote(
            q_ref, queries.at[x], q_send_sem.at[i], q_recv_sem.at[i], x_peer(i)
        )

    def g_copy(i):
        return remote(
            heads_grad.at[x], heads_grad.at[x], g_send_sem.at[i], g_recv_sem.at[i], x_peer(i)
        )

    def h_copy(i):
        return remote(
            hg_send.at[i], hg_recv.at[i], h_send_sem.at[i], h_recv_sem.at[i], m_peer(i)
        )

    def s_copy(i):
        return remote(stat_send, stat_recv.at[i], s_send_sem.at[i], s_recv_sem.at[i], x_peer(i))

    def n_copy(i):
        return remote(
            num_send.at[(x + i) % X], num_recv.at[i], n_send_sem.at[i], n_recv_sem.at[i], x_peer(i)
        )

    def a_copy(i):
        return remote(heads.at[m], heads.at[m], a_send_sem.at[i], a_recv_sem.at[i], m_peer(i))

    def ring_hop(way, kind, half, dist):
        span = pl.ds(half * BLOCK, BLOCK)
        return remote(
            ring_send.at[way, dist, kind, span],
            ring_recv.at[way, dist - 1, kind, span],
            ag_send_sem.at[way, dist, 2 * kind + half],
            rs_recv_sem.at[way, dist, 2 * kind + half],
            toward[way],
        )

    w_copy = pltpu.make_async_copy(w_hbm, w_ref, local_sem.at[0])
    og_copy = pltpu.make_async_copy(og_hbm, og_ref, local_sem.at[1])
    table_copy = pltpu.make_async_copy(codes, table, local_sem.at[2])
    attn_copy = pltpu.make_async_copy(attn_ref, attn_hbm, local_sem.at[3])
    og_copy.start()
    w_copy.start()
    barrier = pltpu.get_barrier_semaphore()
    partners = [right, left] + [x_peer(i) for i in range(1, X)] + [m_peer(i) for i in range(1, M)]
    for partner in partners:
        pl.semaphore_signal(
            barrier, inc=1, device_id=partner, device_id_type=pl.DeviceIdType.MESH
        )
    for kind in (KEY, VALUE):
        own = bank_ref[pl.ds(kind, 2 * BLOCK, stride=2), :].astype(jnp.bfloat16)
        slab[RIGHT, 0, kind] = own
        slab[LEFT, 0, kind] = own
        slab[LEFT, H, kind] = own
    queries[x] = q_ref[...]
    pl.semaphore_wait(barrier, len(partners))

    near = [i for i in range(1, X) if i in (1, X - 1)]
    far = [i for i in range(1, X) if i not in near]
    order = [0] + near + far
    for kind in (KEY, VALUE):
        for half in range(2):
            for way in (RIGHT, LEFT):
                gather_hop(way, kind, half, 1).start()
    for i in order[1:]:
        q_copy(i).start()

    og_copy.wait()
    og = og_ref[...].T
    w_copy.wait()

    def share(i):
        target = (m + i) % M
        band = pl.ds(pl.multiple_of(target * (group * HD), group * HD), group * HD)
        hg_send[i] = dot(og, w_ref[:, band], NN).astype(jnp.bfloat16)

    for i in range(1, M):
        share(i)
        h_copy(i).start()
    share(0)

    numer[...] = jnp.zeros_like(numer)
    denom[...] = jnp.zeros_like(denom)
    key_pos = lax.broadcasted_iota(jnp.int32, (tokens, tokens), 0)
    query_pos = lax.broadcasted_iota(jnp.int32, (tokens, tokens), 1)
    causal = key_pos <= query_pos
    for g in range(group):
        lanes = slice(g * HD, (g + 1) * HD)
        score = dot(k_ref[...], q_ref[:, lanes], NT)
        exp = jnp.exp(softcap * jnp.tanh(score * (qscale / softcap)))
        exp = jnp.where(causal, exp, 0.0)
        denom[x, g : g + 1, :] = jnp.sum(exp, axis=0, keepdims=True)
        numer[x, lanes, :] = dot(v_ref[...], exp.astype(jnp.bfloat16), TN)

    lists = lists_ref[...]
    request_lane = lax.broadcasted_iota(jnp.int32, lists.shape, 1)
    wide = (lists.shape[0], HD)
    entry = lax.broadcasted_iota(jnp.int32, wide, 0)
    lane = lax.broadcasted_iota(jnp.int32, wide, 1)
    is_ahead = lane >= AHEAD
    place = jnp.where(is_ahead, lane - AHEAD, lane)
    spot = jnp.where(is_ahead, jnp.where(place == H, z, z + place), z - place + Z)
    spot = jnp.where(spot >= Z, spot - Z, spot)
    owner = spot * X + x
    for r in range(X):
        column = jnp.sum(
            jnp.where(request_lane == z * X + r, lists, 0), axis=1, keepdims=True
        )
        hit = (entry < block_count[z * X + r]) & (lax.shift_right_logical(column, 1) == owner)
        codes[r : r + 1, :] = jnp.sum(
            jnp.where(hit, 1 + (column & 1), 0), axis=0, keepdims=True
        )
    table_copy.start()
    table_copy.wait()

    def pick(code, way, step, kind):
        return choose(
            code == 2, slab[way, step, kind, BLOCK:, :], slab[way, step, kind, :BLOCK, :]
        )

    def forward(step, offsets):
        for offset in offsets:
            r = (x + offset) % X
            code_a, code_b = table[r, step], table[r, AHEAD + step]
            keys = jnp.concatenate(
                [pick(code_a, 0, step, KEY), pick(code_b, 1, step, KEY)], axis=0
            )
            val_a, val_b = pick(code_a, 0, step, VALUE), pick(code_b, 1, step, VALUE)
            zero = jnp.zeros_like(val_a)
            vals = jnp.concatenate(
                [choose(code_a > 0, val_a, zero), choose(code_b > 0, val_b, zero)], axis=0
            )
            halves = []
            for g in range(group):
                lanes = slice(g * HD, (g + 1) * HD)
                tanh = jnp.tanh(dot(keys, queries[r, :, lanes], NT) * (qscale / softcap))
                exp = jnp.exp(softcap * tanh)
                half = exp.astype(jnp.bfloat16)
                halves.append(half)
                exps[step - 1, r, g] = half
                slopes[step - 1, r, g] = (exp * (1.0 - tanh * tanh)).astype(jnp.bfloat16)
                sum_a = jnp.sum(exp[:BLOCK], axis=0, keepdims=True)
                sum_b = jnp.sum(exp[BLOCK:], axis=0, keepdims=True)
                none = jnp.zeros_like(sum_a)
                denom[r, g : g + 1, :] += choose(code_a > 0, sum_a, none) + choose(
                    code_b > 0, sum_b, none
                )
            mixed = dot(vals, jnp.concatenate(halves, axis=1), TN)
            for g in range(group):
                numer[r, g * HD : (g + 1) * HD, :] += mixed[:, g * tokens : (g + 1) * tokens]

    live = lax.broadcasted_iota(jnp.int32, (group * HD, tokens), 1) < token_count[0]
    early, late = order[: X // 2], order[X // 2 :]

    def pass_on(step, kind):
        for half in range(2):
            for way in (RIGHT, LEFT):
                last = last_hop(way, kind)

                @pl.when(step <= last)
                def _():
                    gather_hop(way, kind, half, step).wait_recv()

                @pl.when(step < last)
                def _():
                    gather_hop(way, kind, half, step + 1).start()

    def gather_step(step, carry):
        @pl.when(step <= H)
        def _():
            pass_on(step, KEY)

        @pl.when(step == 2)
        def _():
            for i in late:
                q_copy(X - i).wait_recv()

        @pl.when(step > 1)
        def _():
            forward(step - 1, late)

        @pl.when(step <= H)
        def _():
            pass_on(step, VALUE)

        @pl.when(step == 1)
        def _():
            for i in early[1:]:
                q_copy(X - i).wait_recv()

        @pl.when(step <= H)
        def _():
            forward(step, early)

        @pl.when(step == min(6, H))
        def _():
            total = hg_send[0].astype(jnp.float32)
            for i in range(1, M):
                h_copy(i).wait_recv()
                total += hg_recv[i].astype(jnp.float32)
            heads_grad[x] = jnp.where(live, total.T, 0.0).astype(jnp.bfloat16)
            for i in order[1:]:
                g_copy(i).start()

        return carry

    lax.fori_loop(1, H + 2, gather_step, 0)

    for i in range(1, X):
        g_copy(i).wait_recv()
    for r in range(X):
        for g in range(group):
            lanes = slice(g * HD, (g + 1) * HD)
            row = (r * group + g) * 2
            stat_send[row : row + 1, :] = denom[r, g : g + 1, :]
            stat_send[row + 1 : row + 2, :] = jnp.sum(
                heads_grad[r, lanes, :].astype(jnp.float32) * numer[r, lanes, :],
                axis=0,
                keepdims=True,
            )
    for i in order[1:]:
        s_copy(i).start()
    num_send[...] = numer[...].astype(jnp.bfloat16)
    for i in order[1:]:
        n_copy(i).start()
    ring_recv[RIGHT, H - 1, VALUE] = jnp.zeros_like(ring_recv[RIGHT, H - 1, VALUE])
    ring_recv[LEFT, H - 1, KEY] = jnp.zeros_like(ring_recv[LEFT, H - 1, KEY])
    stats = stat_send[...]
    for i in range(1, X):
        s_copy(i).wait_recv()
        stats += stat_recv[i]
    for r in range(X):
        for g in range(group):
            lanes = slice(g * HD, (g + 1) * HD)
            row = (r * group + g) * 2
            inverse = 1.0 / stats[row : row + 1, :]
            rows[r, 2 * g : 2 * g + 1, :] = inverse
            rows[r, 2 * g + 1 : 2 * g + 2, :] = inverse * stats[row + 1 : row + 2, :]
            scaled_grad[r, lanes, :] = (
                heads_grad[r, lanes, :].astype(jnp.float32) * inverse
            ).astype(jnp.bfloat16)

    for kind in (KEY, VALUE):
        for way in (RIGHT, LEFT):
            for hop in range(1, last_hop(way, kind) + 1):
                for half in range(2):
                    gather_hop(way, kind, half, hop).wait_send()

    def backward(dist, requests, first):
        slot = dist % 2
        found = []
        for r in requests:
            code_a, code_b = table[r, dist], table[r, AHEAD + dist]
            vals = jnp.concatenate(
                [pick(code_a, 0, dist, VALUE), pick(code_b, 1, dist, VALUE)], axis=0
            )
            key_grad = jnp.zeros((2 * BLOCK, HD), jnp.float32)
            value_grad = jnp.zeros((2 * BLOCK, HD), jnp.float32)
            for g in range(group):
                lanes = slice(g * HD, (g + 1) * HD)
                inverse = rows[r, 2 * g : 2 * g + 1, :]
                delta = rows[r, 2 * g + 1 : 2 * g + 2, :]
                dprob = dot(vals, heads_grad[r, lanes, :], NN)
                slope = slopes[dist - 1, r, g].astype(jnp.float32)
                dscore = slope * ((dprob - delta) * (inverse * qscale))
                key_grad += dot(dscore.astype(jnp.bfloat16), queries[r, :, lanes], NN)
                value_grad += dot(exps[dist - 1, r, g], scaled_grad[r, lanes, :], NT)
            found.append(((code_a, code_b), (key_grad, value_grad)))
        none = jnp.zeros((BLOCK, HD), jnp.float32)
        for side in range(2):
            span = slice(side * BLOCK, (side + 1) * BLOCK)
            for kind in (KEY, VALUE):
                for block in range(2):
                    place = slice(block * BLOCK, (block + 1) * BLOCK)
                    total = none if first else part[slot, side, kind, place, :]
                    for codes, grads in found:
                        total += choose(codes[side] == block + 1, grads[kind][span], none)
                    part[slot, side, kind, place, :] = total

    def hand_over(dist, kind):
        slot = dist % 2
        for half in range(2):
            span = slice(half * BLOCK, (half + 1) * BLOCK)
            for way in (RIGHT, LEFT):
                last = last_hop(way, kind)
                side = 1 - way

                @pl.when(dist == H)
                def _():
                    if way == kind:
                        ring_send[way, H, kind, span, :] = part[slot, 0, kind, span, :].astype(
                            jnp.bfloat16
                        )
                        ring_hop(way, kind, half, H).start()

                @pl.when(dist < H)
                def _():
                    @pl.when(dist < last)
                    def _():
                        ring_hop(way, kind, half, dist + 1).wait_recv()

                    ring_send[way, dist, kind, span, :] = (
                        part[slot, side, kind, span, :]
                        + ring_recv[way, dist, kind, span, :].astype(jnp.float32)
                    ).astype(jnp.bfloat16)
                    ring_hop(way, kind, half, dist).start()

    def scatter_step(index, carry):
        dist = H + 1 - index

        @pl.when(dist <= H)
        def _():
            hand_over(dist, KEY)

        @pl.when(dist > 1)
        def _():
            backward(dist - 1, range(X // 2), True)

        @pl.when(dist <= H)
        def _():
            hand_over(dist, VALUE)

        @pl.when(dist > 1)
        def _():
            backward(dist - 1, range(X // 2, X), False)

        @pl.when(index == 0)
        def _():
            own_sum[...] = part[H % 2, 1]

        @pl.when(index == min(4, H))
        def _():
            total = numer[x]
            for i in range(1, X):
                n_copy(i).wait_recv()
                total += num_recv[i].astype(jnp.float32)
            out = jnp.concatenate(
                [total[g * HD : (g + 1) * HD] * rows[x, 2 * g : 2 * g + 1, :] for g in range(group)],
                axis=0,
            )
            heads[m] = jnp.where(live, out, 0.0).astype(jnp.bfloat16)
            for i in range(1, M):
                a_copy(i).start()

        return carry

    lax.fori_loop(0, H + 1, scatter_step, 0)

    for i in range(1, M):
        a_copy(i).wait_recv()
    depth = group * HD
    total = dot(w_ref[:, :depth], heads[0], NN)
    for j in range(1, M):
        total += dot(w_ref[:, j * depth : (j + 1) * depth], heads[j], NN)
    attn_ref[...] = total
    attn_copy.start()

    for kind in (KEY, VALUE):
        for half in range(2):
            for way in (RIGHT, LEFT):
                ring_hop(way, kind, half, 1).wait_recv()
        total = own_sum[kind]
        for way in (RIGHT, LEFT):
            total += ring_recv[way, 0, kind].astype(jnp.float32)
        grad_ref[pl.ds(kind, 2 * BLOCK, stride=2), :] = total

    for kind in (KEY, VALUE):
        for way in (RIGHT, LEFT):
            for hop in range(1, last_hop(way, kind) + 1):
                for half in range(2):
                    ring_hop(way, kind, half, hop).wait_send()
    attn_copy.wait()
    for i in range(1, X):
        q_copy(i).wait_send()
        g_copy(i).wait_send()
        s_copy(i).wait_send()
        n_copy(i).wait_send()
    for i in range(1, M):
        h_copy(i).wait_send()
        a_copy(i).wait_send()


def local(
    Z,
    X,
    queries,
    keys,
    values,
    out_weight,
    out_grad,
    bank,
    moment_one,
    moment_two,
    block_list,
    block_count,
    token_count,
):
    M = lax.axis_size("mp")
    H = Z // 2
    tokens, heads_width = queries.shape
    group = heads_width // HD
    width = out_weight.shape[1]

    flat = (2 * bank.shape[0], HD)
    bf16, f32 = jnp.bfloat16, jnp.float32
    rows_local = bank.shape[0]
    vmem = pltpu.VMEM
    dma = pltpu.SemaphoreType.DMA
    smem_spec = pl.BlockSpec(memory_space=pltpu.SMEM)
    vmem_spec = pl.BlockSpec(memory_space=pltpu.VMEM)
    any_spec = pl.BlockSpec(memory_space=pl.ANY)
    attn_out, grad = pl.pallas_call(
        functools.partial(step_kernel, (Z, X, M)),
        out_shape=(
            jax.ShapeDtypeStruct((width, tokens), f32),
            jax.ShapeDtypeStruct(flat, f32),
        ),
        in_specs=[smem_spec, smem_spec] + [vmem_spec] * 5 + [any_spec] * 2,
        out_specs=(any_spec, vmem_spec),
        scratch_shapes=[
            vmem((width, out_weight.shape[0]), bf16),
            vmem((width, tokens), bf16),
            vmem((width, tokens), f32),
            vmem((X, HD), jnp.int32),
            pltpu.SMEM((X, HD), jnp.int32),
            vmem((2, H + 1, 2, rows_local, HD), bf16),
            vmem((X, tokens, heads_width), bf16),
            vmem((X, heads_width, tokens), bf16),
            vmem((X, heads_width, tokens), bf16),
            vmem((H, X, group, 2 * BLOCK, tokens), bf16),
            vmem((H, X, group, 2 * BLOCK, tokens), bf16),
            vmem((X, heads_width, tokens), f32),
            vmem((X, group, tokens), f32),
            vmem((M, tokens, heads_width), bf16),
            vmem((M, tokens, heads_width), bf16),
            vmem((2 * X * group, tokens), f32),
            vmem((X, 2 * X * group, tokens), f32),
            vmem((X, 2 * group, tokens), f32),
            vmem((X, heads_width, tokens), bf16),
            vmem((X, heads_width, tokens), bf16),
            vmem((M, heads_width, tokens), bf16),
            vmem((2, 2, 2, rows_local, HD), f32),
            vmem((2, rows_local, HD), f32),
            vmem((2, H + 1, 2, rows_local, HD), bf16),
            vmem((2, H + 1, 2, rows_local, HD), bf16),
            dma((2, H + 1, 4)),
            dma((2, H + 1, 4)),
            dma((X,)),
            dma((X,)),
            dma((X,)),
            dma((X,)),
            dma((M,)),
            dma((M,)),
            dma((X,)),
            dma((X,)),
            dma((X,)),
            dma((X,)),
            dma((M,)),
            dma((M,)),
            dma((2, H + 1, 4)),
            dma((4,)),
        ],
        compiler_params=pltpu.CompilerParams(
            collective_id=0, has_side_effects=True, vmem_limit_bytes=56 << 20
        ),
    )(
        block_count,
        token_count,
        block_list.T,
        bank.reshape(flat),
        queries,
        keys,
        values,
        out_weight.T,
        out_grad.T,
    )

    grad, bank, one, two = lax.optimization_barrier(
        (grad, bank, moment_one.reshape(flat), moment_two.reshape(flat))
    )
    moment_next = beta_one * one + (1.0 - beta_one) * grad
    second_next = beta_two * two + (1.0 - beta_two) * grad * grad
    bank_next = bank.reshape(flat) - learn_rate * (moment_next / bias_one) / (
        jnp.sqrt(second_next / bias_two) + adam_eps
    )
    return (
        attn_out.T,
        bank_next.reshape(bank.shape),
        moment_next.reshape(bank.shape),
        second_next.reshape(bank.shape),
    )


def solution(mesh):
    reqs = mesh.shape["req"]
    X = 4 if reqs >= 64 else 2
    return jax.shard_map(
        functools.partial(local, reqs // X, X),
        mesh=mesh,
        in_specs=(
            P("req", "mp"),
            P("req", "mp"),
            P("req", "mp"),
            P(None, "mp"),
            P("req", "mp"),
            P("req", None, "mp"),
            P("req", None, "mp"),
            P("req", None, "mp"),
            P(),
            P(),
            P("req"),
        ),
        out_specs=(
            P("req", "mp"),
            P("req", None, "mp"),
            P("req", None, "mp"),
            P("req", None, "mp"),
        ),
        check_vma=False,
    )
```

```python
import functools

import jax
import jax.numpy as jnp
from jax import lax
from jax.experimental import pallas as pl
from jax.experimental.pallas import tpu as pltpu
from jax.sharding import PartitionSpec as P

HD = 128
BLOCK = 128
KEY, VALUE = 0, 1
RIGHT, LEFT = 0, 1
AHEAD = 64

softcap = 50.0
qscale = 1.0 / 12.0
beta_one = 0.9
beta_two = 0.999
learn_rate = 0.3
adam_eps = 1e-08
bias_one = 1.0 - 0.9**10
bias_two = 1.0 - 0.999**10

NN = (((1,), (0,)), ((), ()))
NT = (((1,), (1,)), ((), ()))
TN = (((0,), (0,)), ((), ()))


def dot(a, b, dims):
    return lax.dot_general(a, b, dims, preferred_element_type=jnp.float32)


def choose(flag, a, b):
    return lax.select(flag, a, b)


def step_kernel(
    sizes,
    block_count,
    token_count,
    lists_ref,
    bank_ref,
    q_ref,
    k_ref,
    v_ref,
    w_hbm,
    og_hbm,
    attn_hbm,
    grad_ref,
    w_ref,
    og_ref,
    attn_ref,
    codes,
    table,
    slab,
    queries,
    heads_grad,
    scaled_grad,
    exps,
    slopes,
    numer,
    denom,
    hg_send,
    hg_recv,
    stat_send,
    stat_recv,
    rows,
    num_send,
    num_recv,
    heads,
    part,
    own_sum,
    ring_send,
    ring_recv,
    ring_send_sem,
    ag_recv_sem,
    q_send_sem,
    q_recv_sem,
    g_send_sem,
    g_recv_sem,
    h_send_sem,
    h_recv_sem,
    s_send_sem,
    s_recv_sem,
    n_send_sem,
    n_recv_sem,
    a_send_sem,
    a_recv_sem,
    rs_recv_sem,
    local_sem,
):
    Z, X, M = sizes
    H = Z // 2
    tokens = q_ref.shape[0]
    group = q_ref.shape[1] // HD
    req, m = lax.axis_index("req"), lax.axis_index("mp")
    z, x = req // X, req % X
    right = {"req": ((z + 1) % Z) * X + x}
    left = {"req": ((z + Z - 1) % Z) * X + x}
    toward = (right, left)

    def x_peer(i):
        return {"req": z * X + (x + i) % X}

    def m_peer(i):
        return {"mp": (m + i) % M}

    def remote(src, dst, send_sem, recv_sem, device):
        return pltpu.make_async_remote_copy(
            src_ref=src,
            dst_ref=dst,
            send_sem=send_sem,
            recv_sem=recv_sem,
            device_id=device,
            device_id_type=pl.DeviceIdType.MESH,
        )

    def gather_hop(way, kind, half, hop):
        lane = way
        if way == LEFT and kind == VALUE:
            lane = 1 - hop // H
        span = pl.ds(half * BLOCK, BLOCK)
        return remote(
            slab.at[way, hop - 1, kind, span],
            slab.at[lane, hop, kind, span],
            ring_send_sem.at[way, hop % 2, 2 * kind + half],
            ag_recv_sem.at[way, hop, 2 * kind + half],
            toward[way],
        )

    def last_hop(way, kind):
        return H if way == kind else H - 1

    def q_copy(i):
        return remote(
            q_ref, queries.at[x], q_send_sem.at[i], q_recv_sem.at[i], x_peer(i)
        )

    def g_copy(i):
        return remote(
            heads_grad.at[x], heads_grad.at[x], g_send_sem.at[i], g_recv_sem.at[i], x_peer(i)
        )

    def h_copy(i):
        return remote(
            hg_send.at[i], hg_recv.at[i], h_send_sem.at[i], h_recv_sem.at[i], m_peer(i)
        )

    def s_copy(i):
        return remote(stat_send, stat_recv.at[i], s_send_sem.at[i], s_recv_sem.at[i], x_peer(i))

    def n_copy(i):
        return remote(
            num_send.at[(x + i) % X], num_recv.at[i], n_send_sem.at[i], n_recv_sem.at[i], x_peer(i)
        )

    def a_copy(i):
        return remote(heads.at[m], heads.at[m], a_send_sem.at[i], a_recv_sem.at[i], m_peer(i))

    def ring_hop(way, kind, half, dist):
        span = pl.ds(half * BLOCK, BLOCK)
        return remote(
            ring_send.at[way, dist, kind, span],
            ring_recv.at[way, dist - 1, kind, span],
            ring_send_sem.at[way, dist % 2, 2 * kind + half],
            rs_recv_sem.at[way, dist, 2 * kind + half],
            toward[way],
        )

    w_copy = pltpu.make_async_copy(w_hbm, w_ref, local_sem.at[0])
    og_copy = pltpu.make_async_copy(og_hbm, og_ref, local_sem.at[1])
    table_copy = pltpu.make_async_copy(codes, table, local_sem.at[2])
    attn_copy = pltpu.make_async_copy(attn_ref, attn_hbm, local_sem.at[3])
    og_copy.start()
    w_copy.start()
    barrier = pltpu.get_barrier_semaphore()
    partners = [right, left] + [x_peer(i) for i in range(1, X)] + [m_peer(i) for i in range(1, M)]
    for partner in partners:
        pl.semaphore_signal(
            barrier, inc=1, device_id=partner, device_id_type=pl.DeviceIdType.MESH
        )
    for kind in (KEY, VALUE):
        own = bank_ref[pl.ds(kind, 2 * BLOCK, stride=2), :].astype(jnp.bfloat16)
        slab[RIGHT, 0, kind] = own
        slab[LEFT, 0, kind] = own
        slab[LEFT, H, kind] = own
    queries[x] = q_ref[...]
    pl.semaphore_wait(barrier, len(partners))

    near = [i for i in range(1, X) if i in (1, X - 1)]
    far = [i for i in range(1, X) if i not in near]
    order = [0] + near + far
    for kind in (KEY, VALUE):
        for half in range(2):
            for way in (RIGHT, LEFT):
                gather_hop(way, kind, half, 1).start()
    for i in order[1:]:
        q_copy(i).start()

    og_copy.wait()
    og = og_ref[...].T
    w_copy.wait()

    def share(i):
        target = (m + i) % M
        band = pl.ds(pl.multiple_of(target * (group * HD), group * HD), group * HD)
        hg_send[i] = dot(og, w_ref[:, band], NN).astype(jnp.bfloat16)

    for i in range(1, M):
        share(i)
        h_copy(i).start()
    share(0)

    numer[...] = jnp.zeros_like(numer)
    denom[...] = jnp.zeros_like(denom)
    key_pos = lax.broadcasted_iota(jnp.int32, (tokens, tokens), 0)
    query_pos = lax.broadcasted_iota(jnp.int32, (tokens, tokens), 1)
    causal = key_pos <= query_pos
    for g in range(group):
        lanes = slice(g * HD, (g + 1) * HD)
        score = dot(k_ref[...], q_ref[:, lanes], NT)
        exp = jnp.exp(softcap * jnp.tanh(score * (qscale / softcap)))
        exp = jnp.where(causal, exp, 0.0)
        denom[x, g : g + 1, :] = jnp.sum(exp, axis=0, keepdims=True)
        numer[x, lanes, :] = dot(v_ref[...], exp.astype(jnp.bfloat16), TN)

    lists = lists_ref[...]
    request_lane = lax.broadcasted_iota(jnp.int32, lists.shape, 1)
    wide = (lists.shape[0], HD)
    entry = lax.broadcasted_iota(jnp.int32, wide, 0)
    lane = lax.broadcasted_iota(jnp.int32, wide, 1)
    is_ahead = lane >= AHEAD
    place = jnp.where(is_ahead, lane - AHEAD, lane)
    spot = jnp.where(is_ahead, jnp.where(place == H, z, z + place), z - place + Z)
    spot = jnp.where(spot >= Z, spot - Z, spot)
    owner = spot * X + x
    for r in range(X):
        column = jnp.sum(
            jnp.where(request_lane == z * X + r, lists, 0), axis=1, keepdims=True
        )
        hit = (entry < block_count[z * X + r]) & (lax.shift_right_logical(column, 1) == owner)
        codes[r : r + 1, :] = jnp.sum(
            jnp.where(hit, 1 + (column & 1), 0), axis=0, keepdims=True
        )
    table_copy.start()
    table_copy.wait()

    def pick(code, way, step, kind):
        return choose(
            code == 2, slab[way, step, kind, BLOCK:, :], slab[way, step, kind, :BLOCK, :]
        )

    def forward(step, offsets):
        for offset in offsets:
            r = (x + offset) % X
            code_a, code_b = table[r, step], table[r, AHEAD + step]
            keys = jnp.concatenate(
                [pick(code_a, 0, step, KEY), pick(code_b, 1, step, KEY)], axis=0
            )
            val_a, val_b = pick(code_a, 0, step, VALUE), pick(code_b, 1, step, VALUE)
            zero = jnp.zeros_like(val_a)
            vals = jnp.concatenate(
                [choose(code_a > 0, val_a, zero), choose(code_b > 0, val_b, zero)], axis=0
            )
            halves = []
            for g in range(group):
                lanes = slice(g * HD, (g + 1) * HD)
                tanh = jnp.tanh(dot(keys, queries[r, :, lanes], NT) * (qscale / softcap))
                exp = jnp.exp(softcap * tanh)
                half = exp.astype(jnp.bfloat16)
                halves.append(half)
                exps[step - 1, r, g] = half
                slopes[step - 1, r, g] = (exp * (1.0 - tanh * tanh)).astype(jnp.bfloat16)
                sum_a = jnp.sum(exp[:BLOCK], axis=0, keepdims=True)
                sum_b = jnp.sum(exp[BLOCK:], axis=0, keepdims=True)
                none = jnp.zeros_like(sum_a)
                denom[r, g : g + 1, :] += choose(code_a > 0, sum_a, none) + choose(
                    code_b > 0, sum_b, none
                )
            mixed = dot(vals, jnp.concatenate(halves, axis=1), TN)
            for g in range(group):
                numer[r, g * HD : (g + 1) * HD, :] += mixed[:, g * tokens : (g + 1) * tokens]

    live = lax.broadcasted_iota(jnp.int32, (group * HD, tokens), 1) < token_count[0]
    early, late = order[: X // 2], order[X // 2 :]

    def pass_on(step, kind):
        for half in range(2):
            for way in (RIGHT, LEFT):
                last = last_hop(way, kind)

                @pl.when(step <= last)
                def _():
                    gather_hop(way, kind, half, step).wait_recv()

                @pl.when((step < last) & (step > 1))
                def _():
                    gather_hop(way, kind, half, step - 1).wait_send()

                @pl.when(step < last)
                def _():
                    gather_hop(way, kind, half, step + 1).start()

    def gather_step(step, carry):
        @pl.when(step <= H)
        def _():
            pass_on(step, KEY)

        @pl.when(step == 2)
        def _():
            for i in late:
                q_copy(X - i).wait_recv()

        @pl.when(step > 1)
        def _():
            forward(step - 1, late)

        @pl.when(step <= H)
        def _():
            pass_on(step, VALUE)

        @pl.when(step == 1)
        def _():
            for i in early[1:]:
                q_copy(X - i).wait_recv()

        @pl.when(step <= H)
        def _():
            forward(step, early)

        @pl.when(step == min(6, H))
        def _():
            total = hg_send[0].astype(jnp.float32)
            for i in range(1, M):
                h_copy(i).wait_recv()
                total += hg_recv[i].astype(jnp.float32)
            heads_grad[x] = jnp.where(live, total.T, 0.0).astype(jnp.bfloat16)
            for i in order[1:]:
                g_copy(i).start()

        return carry

    lax.fori_loop(1, H + 2, gather_step, 0)

    for i in range(1, X):
        g_copy(i).wait_recv()
    for r in range(X):
        for g in range(group):
            lanes = slice(g * HD, (g + 1) * HD)
            row = (r * group + g) * 2
            stat_send[row : row + 1, :] = denom[r, g : g + 1, :]
            stat_send[row + 1 : row + 2, :] = jnp.sum(
                heads_grad[r, lanes, :].astype(jnp.float32) * numer[r, lanes, :],
                axis=0,
                keepdims=True,
            )
    for i in order[1:]:
        s_copy(i).start()
    num_send[...] = numer[...].astype(jnp.bfloat16)
    for i in order[1:]:
        n_copy(i).start()
    ring_recv[RIGHT, H - 1, VALUE] = jnp.zeros_like(ring_recv[RIGHT, H - 1, VALUE])
    ring_recv[LEFT, H - 1, KEY] = jnp.zeros_like(ring_recv[LEFT, H - 1, KEY])
    for kind in (KEY, VALUE):
        for way in (RIGHT, LEFT):
            last = last_hop(way, kind)
            for hop in range(max(1, last - 1), last + 1):
                for half in range(2):
                    gather_hop(way, kind, half, hop).wait_send()
    for i in range(1, X):
        q_copy(i).wait_send()
        g_copy(i).wait_send()
    for i in range(1, M):
        h_copy(i).wait_send()
    stats = stat_send[...]
    for i in range(1, X):
        s_copy(i).wait_recv()
        stats += stat_recv[i]
    for r in range(X):
        for g in range(group):
            lanes = slice(g * HD, (g + 1) * HD)
            row = (r * group + g) * 2
            inverse = 1.0 / stats[row : row + 1, :]
            rows[r, 2 * g : 2 * g + 1, :] = inverse
            rows[r, 2 * g + 1 : 2 * g + 2, :] = inverse * stats[row + 1 : row + 2, :]
            scaled_grad[r, lanes, :] = (
                heads_grad[r, lanes, :].astype(jnp.float32) * inverse
            ).astype(jnp.bfloat16)

    def backward(dist, requests, first):
        slot = dist % 2
        found = []
        for r in requests:
            code_a, code_b = table[r, dist], table[r, AHEAD + dist]
            vals = jnp.concatenate(
                [pick(code_a, 0, dist, VALUE), pick(code_b, 1, dist, VALUE)], axis=0
            )
            key_grad = jnp.zeros((2 * BLOCK, HD), jnp.float32)
            value_grad = jnp.zeros((2 * BLOCK, HD), jnp.float32)
            for g in range(group):
                lanes = slice(g * HD, (g + 1) * HD)
                inverse = rows[r, 2 * g : 2 * g + 1, :]
                delta = rows[r, 2 * g + 1 : 2 * g + 2, :]
                dprob = dot(vals, heads_grad[r, lanes, :], NN)
                slope = slopes[dist - 1, r, g].astype(jnp.float32)
                dscore = slope * ((dprob - delta) * (inverse * qscale))
                key_grad += dot(dscore.astype(jnp.bfloat16), queries[r, :, lanes], NN)
                value_grad += dot(exps[dist - 1, r, g], scaled_grad[r, lanes, :], NT)
            found.append(((code_a, code_b), (key_grad, value_grad)))
        none = jnp.zeros((BLOCK, HD), jnp.float32)
        for side in range(2):
            span = slice(side * BLOCK, (side + 1) * BLOCK)
            for kind in (KEY, VALUE):
                for block in range(2):
                    place = slice(block * BLOCK, (block + 1) * BLOCK)
                    total = none if first else part[slot, side, kind, place, :]
                    for codes, grads in found:
                        total += choose(codes[side] == block + 1, grads[kind][span], none)
                    part[slot, side, kind, place, :] = total

    def hand_over(dist, kind):
        slot = dist % 2
        for half in range(2):
            span = slice(half * BLOCK, (half + 1) * BLOCK)
            for way in (RIGHT, LEFT):
                last = last_hop(way, kind)
                side = 1 - way

                @pl.when(dist == H)
                def _():
                    if way == kind:
                        ring_send[way, H, kind, span, :] = part[slot, 0, kind, span, :].astype(
                            jnp.bfloat16
                        )
                        ring_hop(way, kind, half, H).start()

                @pl.when(dist < H)
                def _():
                    @pl.when(dist < last)
                    def _():
                        ring_hop(way, kind, half, dist + 1).wait_recv()

                    ring_send[way, dist, kind, span, :] = (
                        part[slot, side, kind, span, :]
                        + ring_recv[way, dist, kind, span, :].astype(jnp.float32)
                    ).astype(jnp.bfloat16)

                    @pl.when(dist + 2 <= last)
                    def _():
                        ring_hop(way, kind, half, dist + 2).wait_send()

                    ring_hop(way, kind, half, dist).start()

    def scatter_step(index, carry):
        dist = H + 1 - index

        @pl.when(dist <= H)
        def _():
            hand_over(dist, KEY)

        @pl.when(dist > 1)
        def _():
            backward(dist - 1, range(X // 2), True)

        @pl.when(dist <= H)
        def _():
            hand_over(dist, VALUE)

        @pl.when(dist > 1)
        def _():
            backward(dist - 1, range(X // 2, X), False)

        @pl.when(index == 0)
        def _():
            own_sum[...] = part[H % 2, 1]

        @pl.when(index == min(4, H))
        def _():
            total = numer[x]
            for i in range(1, X):
                n_copy(i).wait_recv()
                total += num_recv[i].astype(jnp.float32)
            out = jnp.concatenate(
                [total[g * HD : (g + 1) * HD] * rows[x, 2 * g : 2 * g + 1, :] for g in range(group)],
                axis=0,
            )
            heads[m] = jnp.where(live, out, 0.0).astype(jnp.bfloat16)
            for i in range(1, M):
                a_copy(i).start()

        return carry

    lax.fori_loop(0, H + 1, scatter_step, 0)

    for i in range(1, M):
        a_copy(i).wait_recv()
    depth = group * HD
    total = dot(w_ref[:, :depth], heads[0], NN)
    for j in range(1, M):
        total += dot(w_ref[:, j * depth : (j + 1) * depth], heads[j], NN)
    attn_ref[...] = total
    attn_copy.start()
    for i in range(1, X):
        s_copy(i).wait_send()
        n_copy(i).wait_send()
    for i in range(1, M):
        a_copy(i).wait_send()

    for kind in (KEY, VALUE):
        for half in range(2):
            for way in (RIGHT, LEFT):
                ring_hop(way, kind, half, 1).wait_recv()
        total = own_sum[kind]
        for way in (RIGHT, LEFT):
            total += ring_recv[way, 0, kind].astype(jnp.float32)
        grad_ref[pl.ds(kind, 2 * BLOCK, stride=2), :] = total

    for kind in (KEY, VALUE):
        for way in (RIGHT, LEFT):
            for dist in range(1, min(2, last_hop(way, kind)) + 1):
                for half in range(2):
                    ring_hop(way, kind, half, dist).wait_send()
    attn_copy.wait()


def update_kernel(
    grad_ref,
    bank_ref,
    one_ref,
    two_ref,
    attn_ref,
    attn_out,
    bank_out,
    one_out,
    two_out,
    sems,
):
    pieces = sems.shape[0]
    size = attn_ref.shape[0] // pieces
    copies = [
        pltpu.make_async_copy(
            attn_ref.at[pl.ds(i * size, size)], attn_out.at[pl.ds(i * size, size)], sems.at[i]
        )
        for i in range(pieces)
    ]
    for copy in copies:
        copy.start()
    grad = grad_ref[...]
    moment_next = beta_one * one_ref[...] + (1.0 - beta_one) * grad
    second_next = beta_two * two_ref[...] + (1.0 - beta_two) * grad * grad
    one_out[...] = moment_next
    two_out[...] = second_next
    bank_out[...] = bank_ref[...] - learn_rate * (moment_next / bias_one) / (
        jnp.sqrt(second_next / bias_two) + adam_eps
    )
    for copy in copies:
        copy.wait()


def local(
    Z,
    X,
    queries,
    keys,
    values,
    out_weight,
    out_grad,
    bank,
    moment_one,
    moment_two,
    block_list,
    block_count,
    token_count,
):
    M = lax.axis_size("mp")
    H = Z // 2
    tokens, heads_width = queries.shape
    group = heads_width // HD
    width = out_weight.shape[1]

    flat = (2 * bank.shape[0], HD)
    bf16, f32 = jnp.bfloat16, jnp.float32
    rows_local = bank.shape[0]
    vmem = pltpu.VMEM
    dma = pltpu.SemaphoreType.DMA
    smem_spec = pl.BlockSpec(memory_space=pltpu.SMEM)
    vmem_spec = pl.BlockSpec(memory_space=pltpu.VMEM)
    any_spec = pl.BlockSpec(memory_space=pl.ANY)
    attn_out, grad = pl.pallas_call(
        functools.partial(step_kernel, (Z, X, M)),
        out_shape=(
            jax.ShapeDtypeStruct((width, tokens), f32),
            jax.ShapeDtypeStruct(flat, f32),
        ),
        in_specs=[smem_spec, smem_spec] + [vmem_spec] * 5 + [any_spec] * 2,
        out_specs=(any_spec, vmem_spec),
        scratch_shapes=[
            vmem((width, out_weight.shape[0]), bf16),
            vmem((width, tokens), bf16),
            vmem((width, tokens), f32),
            vmem((X, HD), jnp.int32),
            pltpu.SMEM((X, HD), jnp.int32),
            vmem((2, H + 1, 2, rows_local, HD), bf16),
            vmem((X, tokens, heads_width), bf16),
            vmem((X, heads_width, tokens), bf16),
            vmem((X, heads_width, tokens), bf16),
            vmem((H, X, group, 2 * BLOCK, tokens), bf16),
            vmem((H, X, group, 2 * BLOCK, tokens), bf16),
            vmem((X, heads_width, tokens), f32),
            vmem((X, group, tokens), f32),
            vmem((M, tokens, heads_width), bf16),
            vmem((M, tokens, heads_width), bf16),
            vmem((2 * X * group, tokens), f32),
            vmem((X, 2 * X * group, tokens), f32),
            vmem((X, 2 * group, tokens), f32),
            vmem((X, heads_width, tokens), bf16),
            vmem((X, heads_width, tokens), bf16),
            vmem((M, heads_width, tokens), bf16),
            vmem((2, 2, 2, rows_local, HD), f32),
            vmem((2, rows_local, HD), f32),
            vmem((2, H + 1, 2, rows_local, HD), bf16),
            vmem((2, H + 1, 2, rows_local, HD), bf16),
            dma((2, 2, 4)),
            dma((2, H + 1, 4)),
            dma((X,)),
            dma((X,)),
            dma((X,)),
            dma((X,)),
            dma((M,)),
            dma((M,)),
            dma((X,)),
            dma((X,)),
            dma((X,)),
            dma((X,)),
            dma((M,)),
            dma((M,)),
            dma((2, H + 1, 4)),
            dma((4,)),
        ],
        compiler_params=pltpu.CompilerParams(
            collective_id=0, has_side_effects=True, vmem_limit_bytes=56 << 20
        ),
    )(
        block_count,
        token_count,
        block_list.T,
        bank.reshape(flat),
        queries,
        keys,
        values,
        out_weight.T,
        out_grad.T,
    )

    attn_out, bank_next, moment_next, second_next = pl.pallas_call(
        update_kernel,
        out_shape=(jax.ShapeDtypeStruct((width, tokens), f32),)
        + (jax.ShapeDtypeStruct(flat, f32),) * 3,
        in_specs=[vmem_spec] * 4 + [any_spec],
        out_specs=(any_spec,) + (vmem_spec,) * 3,
        scratch_shapes=[dma((4,))],
    )(grad, bank.reshape(flat), moment_one.reshape(flat), moment_two.reshape(flat), attn_out)
    return (
        attn_out.T,
        bank_next.reshape(bank.shape),
        moment_next.reshape(bank.shape),
        second_next.reshape(bank.shape),
    )


def solution(mesh):
    reqs = mesh.shape["req"]
    X = 4 if reqs >= 64 else 2
    return jax.shard_map(
        functools.partial(local, reqs // X, X),
        mesh=mesh,
        in_specs=(
            P("req", "mp"),
            P("req", "mp"),
            P("req", "mp"),
            P(None, "mp"),
            P("req", "mp"),
            P("req", None, "mp"),
            P("req", None, "mp"),
            P("req", None, "mp"),
            P(),
            P(),
            P("req"),
        ),
        out_specs=(
            P("req", "mp"),
            P("req", None, "mp"),
            P("req", None, "mp"),
            P("req", None, "mp"),
        ),
        check_vma=False,
    )
```

```python
import functools

import jax
import jax.numpy as jnp
from jax import lax
from jax.experimental import pallas as pl
from jax.experimental.pallas import tpu as pltpu
from jax.sharding import PartitionSpec as P

HD = 128
BLOCK = 128
KEY, VALUE = 0, 1
RIGHT, LEFT = 0, 1
AHEAD = 64

softcap = 50.0
qscale = 1.0 / 12.0
beta_one = 0.9
beta_two = 0.999
learn_rate = 0.3
adam_eps = 1e-08
bias_one = 1.0 - 0.9**10
bias_two = 1.0 - 0.999**10

NN = (((1,), (0,)), ((), ()))
NT = (((1,), (1,)), ((), ()))
TN = (((0,), (0,)), ((), ()))


def dot(a, b, dims):
    return lax.dot_general(a, b, dims, preferred_element_type=jnp.float32)


def choose(flag, a, b):
    return lax.select(flag, a, b)


def step_kernel(
    sizes,
    block_count,
    token_count,
    lists_ref,
    bank_ref,
    q_ref,
    k_ref,
    v_ref,
    w_hbm,
    og_hbm,
    attn_hbm,
    grad_ref,
    w_ref,
    og_ref,
    attn_ref,
    codes,
    table,
    slab,
    queries,
    heads_grad,
    scaled_grad,
    exps,
    slopes,
    numer,
    denom,
    hg_send,
    hg_recv,
    stat_send,
    stat_recv,
    rows,
    num_send,
    num_recv,
    heads,
    part,
    own_sum,
    ring_send,
    ring_recv,
    ring_send_sem,
    ag_recv_sem,
    q_send_sem,
    q_recv_sem,
    g_send_sem,
    g_recv_sem,
    h_send_sem,
    h_recv_sem,
    s_send_sem,
    s_recv_sem,
    n_send_sem,
    n_recv_sem,
    a_send_sem,
    a_recv_sem,
    rs_recv_sem,
    local_sem,
):
    Z, X, M = sizes
    H = Z // 2
    tokens = q_ref.shape[0]
    group = q_ref.shape[1] // HD
    req, m = lax.axis_index("req"), lax.axis_index("mp")
    z, x = req // X, req % X
    right = {"req": ((z + 1) % Z) * X + x}
    left = {"req": ((z + Z - 1) % Z) * X + x}
    toward = (right, left)

    def x_peer(i):
        return {"req": z * X + (x + i) % X}

    def m_peer(i):
        return {"mp": (m + i) % M}

    def remote(src, dst, send_sem, recv_sem, device):
        return pltpu.make_async_remote_copy(
            src_ref=src,
            dst_ref=dst,
            send_sem=send_sem,
            recv_sem=recv_sem,
            device_id=device,
            device_id_type=pl.DeviceIdType.MESH,
        )

    def gather_hop(way, kind, half, hop):
        lane = way
        if way == LEFT and kind == VALUE:
            lane = 1 - hop // H
        span = pl.ds(half * BLOCK, BLOCK)
        return remote(
            slab.at[way, hop - 1, kind, span],
            slab.at[lane, hop, kind, span],
            ring_send_sem.at[way, hop % 2, 2 * kind + half],
            ag_recv_sem.at[way, hop, 2 * kind + half],
            toward[way],
        )

    def last_hop(way, kind):
        return H if way == kind else H - 1

    def q_copy(i):
        return remote(
            q_ref, queries.at[x], q_send_sem.at[i], q_recv_sem.at[i], x_peer(i)
        )

    def g_copy(i):
        return remote(
            heads_grad.at[x], heads_grad.at[x], g_send_sem.at[i], g_recv_sem.at[i], x_peer(i)
        )

    def h_copy(i):
        return remote(
            hg_send.at[i], hg_recv.at[i], h_send_sem.at[i], h_recv_sem.at[i], m_peer(i)
        )

    def s_copy(i):
        return remote(stat_send, stat_recv.at[i], s_send_sem.at[i], s_recv_sem.at[i], x_peer(i))

    def n_copy(i):
        return remote(
            num_send.at[(x + i) % X], num_recv.at[i], n_send_sem.at[i], n_recv_sem.at[i], x_peer(i)
        )

    def a_copy(i):
        return remote(heads.at[m], heads.at[m], a_send_sem.at[i], a_recv_sem.at[i], m_peer(i))

    def ring_hop(way, kind, half, dist):
        span = pl.ds(half * BLOCK, BLOCK)
        return remote(
            ring_send.at[way, dist, kind, span],
            ring_recv.at[way, dist - 1, kind, span],
            ring_send_sem.at[way, dist % 2, 2 * kind + half],
            rs_recv_sem.at[way, dist, 2 * kind + half],
            toward[way],
        )

    w_copy = pltpu.make_async_copy(w_hbm, w_ref, local_sem.at[0])
    og_copy = pltpu.make_async_copy(og_hbm, og_ref, local_sem.at[1])
    table_copy = pltpu.make_async_copy(codes, table, local_sem.at[2])
    attn_copy = pltpu.make_async_copy(attn_ref, attn_hbm, local_sem.at[3])
    og_copy.start()
    w_copy.start()
    barrier = pltpu.get_barrier_semaphore()
    partners = [right, left] + [x_peer(i) for i in range(1, X)] + [m_peer(i) for i in range(1, M)]
    for partner in partners:
        pl.semaphore_signal(
            barrier, inc=1, device_id=partner, device_id_type=pl.DeviceIdType.MESH
        )
    for kind in (KEY, VALUE):
        own = bank_ref[pl.ds(kind, 2 * BLOCK, stride=2), :].astype(jnp.bfloat16)
        slab[RIGHT, 0, kind] = own
        slab[LEFT, 0, kind] = own
        slab[LEFT, H, kind] = own
    queries[x] = q_ref[...]
    pl.semaphore_wait(barrier, len(partners))

    near = [i for i in range(1, X) if i in (1, X - 1)]
    far = [i for i in range(1, X) if i not in near]
    order = [0] + near + far
    for kind in (KEY, VALUE):
        for half in range(2):
            for way in (RIGHT, LEFT):
                gather_hop(way, kind, half, 1).start()
    for i in order[1:]:
        q_copy(i).start()

    og_copy.wait()
    og = og_ref[...].T
    w_copy.wait()

    def share(i):
        target = (m + i) % M
        band = pl.ds(pl.multiple_of(target * (group * HD), group * HD), group * HD)
        hg_send[i] = dot(og, w_ref[:, band], NN).astype(jnp.bfloat16)

    for i in range(1, M):
        share(i)
        h_copy(i).start()
    share(0)

    numer[...] = jnp.zeros_like(numer)
    denom[...] = jnp.zeros_like(denom)
    key_pos = lax.broadcasted_iota(jnp.int32, (tokens, tokens), 0)
    query_pos = lax.broadcasted_iota(jnp.int32, (tokens, tokens), 1)
    causal = key_pos <= query_pos
    for g in range(group):
        lanes = slice(g * HD, (g + 1) * HD)
        score = dot(k_ref[...], q_ref[:, lanes], NT)
        exp = jnp.exp(softcap * jnp.tanh(score * (qscale / softcap)))
        exp = jnp.where(causal, exp, 0.0)
        denom[x, g : g + 1, :] = jnp.sum(exp, axis=0, keepdims=True)
        numer[x, lanes, :] = dot(v_ref[...], exp.astype(jnp.bfloat16), TN)

    lists = lists_ref[...]
    request_lane = lax.broadcasted_iota(jnp.int32, lists.shape, 1)
    wide = (lists.shape[0], HD)
    entry = lax.broadcasted_iota(jnp.int32, wide, 0)
    lane = lax.broadcasted_iota(jnp.int32, wide, 1)
    is_ahead = lane >= AHEAD
    place = jnp.where(is_ahead, lane - AHEAD, lane)
    spot = jnp.where(is_ahead, jnp.where(place == H, z, z + place), z - place + Z)
    spot = jnp.where(spot >= Z, spot - Z, spot)
    owner = spot * X + x
    for r in range(X):
        column = jnp.sum(
            jnp.where(request_lane == z * X + r, lists, 0), axis=1, keepdims=True
        )
        hit = (entry < block_count[z * X + r]) & (lax.shift_right_logical(column, 1) == owner)
        codes[r : r + 1, :] = jnp.sum(
            jnp.where(hit, 1 + (column & 1), 0), axis=0, keepdims=True
        )
    table_copy.start()
    table_copy.wait()

    def pick(code, way, step, kind):
        return choose(
            code == 2, slab[way, step, kind, BLOCK:, :], slab[way, step, kind, :BLOCK, :]
        )

    def forward(step, offsets):
        for offset in offsets:
            r = (x + offset) % X
            code_a, code_b = table[r, step], table[r, AHEAD + step]
            keys = jnp.concatenate(
                [pick(code_a, 0, step, KEY), pick(code_b, 1, step, KEY)], axis=0
            )
            val_a, val_b = pick(code_a, 0, step, VALUE), pick(code_b, 1, step, VALUE)
            zero = jnp.zeros_like(val_a)
            vals = jnp.concatenate(
                [choose(code_a > 0, val_a, zero), choose(code_b > 0, val_b, zero)], axis=0
            )
            halves = []
            for g in range(group):
                lanes = slice(g * HD, (g + 1) * HD)
                tanh = jnp.tanh(dot(keys, queries[r, :, lanes], NT) * (qscale / softcap))
                exp = jnp.exp(softcap * tanh)
                half = exp.astype(jnp.bfloat16)
                halves.append(half)
                exps[step - 1, r, g] = half
                slopes[step - 1, r, g] = (exp * (1.0 - tanh * tanh)).astype(jnp.bfloat16)
                sum_a = jnp.sum(exp[:BLOCK], axis=0, keepdims=True)
                sum_b = jnp.sum(exp[BLOCK:], axis=0, keepdims=True)
                none = jnp.zeros_like(sum_a)
                denom[r, g : g + 1, :] += choose(code_a > 0, sum_a, none) + choose(
                    code_b > 0, sum_b, none
                )
            mixed = dot(vals, jnp.concatenate(halves, axis=1), TN)
            for g in range(group):
                numer[r, g * HD : (g + 1) * HD, :] += mixed[:, g * tokens : (g + 1) * tokens]

    live = lax.broadcasted_iota(jnp.int32, (group * HD, tokens), 1) < token_count[0]
    early, late = order[: X // 2], order[X // 2 :]

    def pass_on(step, kind):
        for half in range(2):
            for way in (RIGHT, LEFT):
                last = last_hop(way, kind)

                @pl.when(step <= last)
                def _():
                    gather_hop(way, kind, half, step).wait_recv()

                @pl.when((step < last) & (step > 1))
                def _():
                    gather_hop(way, kind, half, step - 1).wait_send()

                @pl.when(step < last)
                def _():
                    gather_hop(way, kind, half, step + 1).start()

    def gather_step(step, carry):
        @pl.when(step <= H)
        def _():
            pass_on(step, KEY)

        @pl.when(step == 2)
        def _():
            for i in late:
                q_copy(X - i).wait_recv()

        @pl.when(step > 1)
        def _():
            forward(step - 1, late)

        @pl.when(step <= H)
        def _():
            pass_on(step, VALUE)

        @pl.when(step == 1)
        def _():
            for i in early[1:]:
                q_copy(X - i).wait_recv()

        @pl.when(step <= H)
        def _():
            forward(step, early)

        @pl.when(step == min(6, H))
        def _():
            total = hg_send[0].astype(jnp.float32)
            for i in range(1, M):
                h_copy(i).wait_recv()
                total += hg_recv[i].astype(jnp.float32)
            heads_grad[x] = jnp.where(live, total.T, 0.0).astype(jnp.bfloat16)
            for i in order[1:]:
                g_copy(i).start()

        return carry

    lax.fori_loop(1, H + 2, gather_step, 0)

    for i in range(1, X):
        g_copy(i).wait_recv()
    for r in range(X):
        for g in range(group):
            lanes = slice(g * HD, (g + 1) * HD)
            row = (r * group + g) * 2
            stat_send[row : row + 1, :] = denom[r, g : g + 1, :]
            stat_send[row + 1 : row + 2, :] = jnp.sum(
                heads_grad[r, lanes, :].astype(jnp.float32) * numer[r, lanes, :],
                axis=0,
                keepdims=True,
            )
    for i in order[1:]:
        s_copy(i).start()
    num_send[...] = numer[...].astype(jnp.bfloat16)
    for i in order[1:]:
        n_copy(i).start()
    ring_recv[RIGHT, H - 1, VALUE] = jnp.zeros_like(ring_recv[RIGHT, H - 1, VALUE])
    ring_recv[LEFT, H - 1, KEY] = jnp.zeros_like(ring_recv[LEFT, H - 1, KEY])
    for kind in (KEY, VALUE):
        for way in (RIGHT, LEFT):
            last = last_hop(way, kind)
            for hop in range(max(1, last - 1), last + 1):
                for half in range(2):
                    gather_hop(way, kind, half, hop).wait_send()
    for i in range(1, X):
        q_copy(i).wait_send()
        g_copy(i).wait_send()
    for i in range(1, M):
        h_copy(i).wait_send()
    stats = stat_send[...]
    for i in range(1, X):
        s_copy(i).wait_recv()
        stats += stat_recv[i]
    for r in range(X):
        for g in range(group):
            lanes = slice(g * HD, (g + 1) * HD)
            row = (r * group + g) * 2
            inverse = 1.0 / stats[row : row + 1, :]
            rows[r, 2 * g : 2 * g + 1, :] = inverse
            rows[r, 2 * g + 1 : 2 * g + 2, :] = inverse * stats[row + 1 : row + 2, :]
            scaled_grad[r, lanes, :] = (
                heads_grad[r, lanes, :].astype(jnp.float32) * inverse
            ).astype(jnp.bfloat16)

    def backward(dist, requests, first):
        slot = dist % 2
        found = []
        for r in requests:
            code_a, code_b = table[r, dist], table[r, AHEAD + dist]
            vals = jnp.concatenate(
                [pick(code_a, 0, dist, VALUE), pick(code_b, 1, dist, VALUE)], axis=0
            )
            key_grad = jnp.zeros((2 * BLOCK, HD), jnp.float32)
            value_grad = jnp.zeros((2 * BLOCK, HD), jnp.float32)
            for g in range(group):
                lanes = slice(g * HD, (g + 1) * HD)
                inverse = rows[r, 2 * g : 2 * g + 1, :]
                delta = rows[r, 2 * g + 1 : 2 * g + 2, :]
                dprob = dot(vals, heads_grad[r, lanes, :], NN)
                slope = slopes[dist - 1, r, g].astype(jnp.float32)
                dscore = slope * ((dprob - delta) * (inverse * qscale))
                key_grad += dot(dscore.astype(jnp.bfloat16), queries[r, :, lanes], NN)
                value_grad += dot(exps[dist - 1, r, g], scaled_grad[r, lanes, :], NT)
            found.append(((code_a, code_b), (key_grad, value_grad)))
        none = jnp.zeros((BLOCK, HD), jnp.float32)
        for side in range(2):
            span = slice(side * BLOCK, (side + 1) * BLOCK)
            for kind in (KEY, VALUE):
                for block in range(2):
                    place = slice(block * BLOCK, (block + 1) * BLOCK)
                    total = none if first else part[slot, side, kind, place, :]
                    for codes, grads in found:
                        total += choose(codes[side] == block + 1, grads[kind][span], none)
                    part[slot, side, kind, place, :] = total

    def hand_over(dist, kind):
        slot = dist % 2
        for half in range(2):
            span = slice(half * BLOCK, (half + 1) * BLOCK)
            for way in (RIGHT, LEFT):
                last = last_hop(way, kind)
                side = 1 - way

                @pl.when(dist == H)
                def _():
                    if way == kind:
                        ring_send[way, H, kind, span, :] = part[slot, 0, kind, span, :].astype(
                            jnp.bfloat16
                        )
                        ring_hop(way, kind, half, H).start()

                @pl.when(dist < H)
                def _():
                    @pl.when(dist < last)
                    def _():
                        ring_hop(way, kind, half, dist + 1).wait_recv()

                    ring_send[way, dist, kind, span, :] = (
                        part[slot, side, kind, span, :]
                        + ring_recv[way, dist, kind, span, :].astype(jnp.float32)
                    ).astype(jnp.bfloat16)

                    @pl.when(dist + 2 <= last)
                    def _():
                        ring_hop(way, kind, half, dist + 2).wait_send()

                    ring_hop(way, kind, half, dist).start()

    def scatter_step(index, carry):
        dist = H + 1 - index

        @pl.when(dist <= H)
        def _():
            hand_over(dist, KEY)

        @pl.when(dist > 1)
        def _():
            backward(dist - 1, range(X // 2), True)

        @pl.when(dist <= H)
        def _():
            hand_over(dist, VALUE)

        @pl.when(dist > 1)
        def _():
            backward(dist - 1, range(X // 2, X), False)

        @pl.when(index == 0)
        def _():
            own_sum[...] = part[H % 2, 1]

        @pl.when(index == min(4, H))
        def _():
            total = numer[x]
            for i in range(1, X):
                n_copy(i).wait_recv()
                total += num_recv[i].astype(jnp.float32)
            out = jnp.concatenate(
                [total[g * HD : (g + 1) * HD] * rows[x, 2 * g : 2 * g + 1, :] for g in range(group)],
                axis=0,
            )
            heads[m] = jnp.where(live, out, 0.0).astype(jnp.bfloat16)
            for i in range(1, M):
                a_copy(i).start()

        return carry

    lax.fori_loop(0, H + 1, scatter_step, 0)

    for i in range(1, M):
        a_copy(i).wait_recv()
    depth = group * HD
    total = dot(w_ref[:, :depth], heads[0], NN)
    for j in range(1, M):
        total += dot(w_ref[:, j * depth : (j + 1) * depth], heads[j], NN)
    attn_ref[...] = total
    attn_copy.start()
    for i in range(1, X):
        s_copy(i).wait_send()
        n_copy(i).wait_send()
    for i in range(1, M):
        a_copy(i).wait_send()

    for kind in (KEY, VALUE):
        for half in range(2):
            for way in (RIGHT, LEFT):
                ring_hop(way, kind, half, 1).wait_recv()
        total = own_sum[kind]
        for way in (RIGHT, LEFT):
            total += ring_recv[way, 0, kind].astype(jnp.float32)
        grad_ref[pl.ds(kind, 2 * BLOCK, stride=2), :] = total

    for kind in (KEY, VALUE):
        for way in (RIGHT, LEFT):
            for dist in range(1, min(2, last_hop(way, kind)) + 1):
                for half in range(2):
                    ring_hop(way, kind, half, dist).wait_send()
    attn_copy.wait()


def update_kernel(
    grad_ref,
    bank_ref,
    one_ref,
    two_ref,
    attn_ref,
    attn_out,
    bank_out,
    one_out,
    two_out,
):
    attn_out[...] = attn_ref[...]
    grad = grad_ref[...]
    moment_next = beta_one * one_ref[...] + (1.0 - beta_one) * grad
    second_next = beta_two * two_ref[...] + (1.0 - beta_two) * grad * grad
    one_out[...] = moment_next
    two_out[...] = second_next
    bank_out[...] = bank_ref[...] - learn_rate * (moment_next / bias_one) / (
        jnp.sqrt(second_next / bias_two) + adam_eps
    )


def local(
    Z,
    X,
    queries,
    keys,
    values,
    out_weight,
    out_grad,
    bank,
    moment_one,
    moment_two,
    block_list,
    block_count,
    token_count,
):
    M = lax.axis_size("mp")
    H = Z // 2
    tokens, heads_width = queries.shape
    group = heads_width // HD
    width = out_weight.shape[1]

    flat = (2 * bank.shape[0], HD)
    bf16, f32 = jnp.bfloat16, jnp.float32
    rows_local = bank.shape[0]
    vmem = pltpu.VMEM
    dma = pltpu.SemaphoreType.DMA
    smem_spec = pl.BlockSpec(memory_space=pltpu.SMEM)
    vmem_spec = pl.BlockSpec(memory_space=pltpu.VMEM)
    any_spec = pl.BlockSpec(memory_space=pl.ANY)
    attn_out, grad = pl.pallas_call(
        functools.partial(step_kernel, (Z, X, M)),
        out_shape=(
            jax.ShapeDtypeStruct((width, tokens), f32),
            jax.ShapeDtypeStruct(flat, f32),
        ),
        in_specs=[smem_spec, smem_spec] + [vmem_spec] * 5 + [any_spec] * 2,
        out_specs=(any_spec, vmem_spec),
        scratch_shapes=[
            vmem((width, out_weight.shape[0]), bf16),
            vmem((width, tokens), bf16),
            vmem((width, tokens), f32),
            vmem((X, HD), jnp.int32),
            pltpu.SMEM((X, HD), jnp.int32),
            vmem((2, H + 1, 2, rows_local, HD), bf16),
            vmem((X, tokens, heads_width), bf16),
            vmem((X, heads_width, tokens), bf16),
            vmem((X, heads_width, tokens), bf16),
            vmem((H, X, group, 2 * BLOCK, tokens), bf16),
            vmem((H, X, group, 2 * BLOCK, tokens), bf16),
            vmem((X, heads_width, tokens), f32),
            vmem((X, group, tokens), f32),
            vmem((M, tokens, heads_width), bf16),
            vmem((M, tokens, heads_width), bf16),
            vmem((2 * X * group, tokens), f32),
            vmem((X, 2 * X * group, tokens), f32),
            vmem((X, 2 * group, tokens), f32),
            vmem((X, heads_width, tokens), bf16),
            vmem((X, heads_width, tokens), bf16),
            vmem((M, heads_width, tokens), bf16),
            vmem((2, 2, 2, rows_local, HD), f32),
            vmem((2, rows_local, HD), f32),
            vmem((2, H + 1, 2, rows_local, HD), bf16),
            vmem((2, H + 1, 2, rows_local, HD), bf16),
            dma((2, 2, 4)),
            dma((2, H + 1, 4)),
            dma((X,)),
            dma((X,)),
            dma((X,)),
            dma((X,)),
            dma((M,)),
            dma((M,)),
            dma((X,)),
            dma((X,)),
            dma((X,)),
            dma((X,)),
            dma((M,)),
            dma((M,)),
            dma((2, H + 1, 4)),
            dma((4,)),
        ],
        compiler_params=pltpu.CompilerParams(
            collective_id=0, has_side_effects=True, vmem_limit_bytes=56 << 20
        ),
    )(
        block_count,
        token_count,
        block_list.T,
        bank.reshape(flat),
        queries,
        keys,
        values,
        out_weight.T,
        out_grad.T,
    )


    def half_rows(rows, columns):
        return pl.BlockSpec((rows // 2, columns), lambda i: (i, 0))

    attn_out, bank_next, moment_next, second_next = pl.pallas_call(
        update_kernel,
        out_shape=(jax.ShapeDtypeStruct((width, tokens), f32),)
        + (jax.ShapeDtypeStruct(flat, f32),) * 3,
        grid=(2,),
        in_specs=[half_rows(*flat)] * 4 + [half_rows(width, tokens)],
        out_specs=(half_rows(width, tokens),) + (half_rows(*flat),) * 3,
    )(grad, bank.reshape(flat), moment_one.reshape(flat), moment_two.reshape(flat), attn_out)
    return (
        attn_out.T,
        bank_next.reshape(bank.shape),
        moment_next.reshape(bank.shape),
        second_next.reshape(bank.shape),
    )


def solution(mesh):
    reqs = mesh.shape["req"]
    X = 4 if reqs >= 64 else 2
    return jax.shard_map(
        functools.partial(local, reqs // X, X),
        mesh=mesh,
        in_specs=(
            P("req", "mp"),
            P("req", "mp"),
            P("req", "mp"),
            P(None, "mp"),
            P("req", "mp"),
            P("req", None, "mp"),
            P("req", None, "mp"),
            P("req", None, "mp"),
            P(),
            P(),
            P("req"),
        ),
        out_specs=(
            P("req", "mp"),
            P("req", None, "mp"),
            P("req", None, "mp"),
            P("req", None, "mp"),
        ),
        check_vma=False,
    )
```

```python
import functools

import jax
import jax.numpy as jnp
from jax import lax
from jax.experimental import pallas as pl
from jax.experimental.pallas import tpu as pltpu
from jax.sharding import PartitionSpec as P

HD = 128
BLOCK = 128
KEY, VALUE = 0, 1
RIGHT, LEFT = 0, 1
AHEAD = 64

softcap = 50.0
qscale = 1.0 / 12.0
beta_one = 0.9
beta_two = 0.999
learn_rate = 0.3
adam_eps = 1e-08
bias_one = 1.0 - 0.9**10
bias_two = 1.0 - 0.999**10

NN = (((1,), (0,)), ((), ()))
NT = (((1,), (1,)), ((), ()))
TN = (((0,), (0,)), ((), ()))


def dot(a, b, dims):
    return lax.dot_general(a, b, dims, preferred_element_type=jnp.float32)


def choose(flag, a, b):
    return lax.select(flag, a, b)


def step_kernel(
    sizes,
    block_count,
    token_count,
    lists_ref,
    bank_ref,
    q_ref,
    k_ref,
    v_ref,
    w_hbm,
    og_hbm,
    attn_hbm,
    grad_ref,
    w_ref,
    og_ref,
    attn_ref,
    codes,
    table,
    slab,
    queries,
    heads_grad,
    scaled_grad,
    exps,
    slopes,
    numer,
    denom,
    hg_send,
    hg_recv,
    stat_send,
    stat_recv,
    rows,
    num_send,
    num_recv,
    heads,
    part,
    own_sum,
    first_prob,
    ring_send,
    ring_recv,
    ring_send_sem,
    ag_recv_sem,
    q_send_sem,
    q_recv_sem,
    g_send_sem,
    g_recv_sem,
    h_send_sem,
    h_recv_sem,
    s_send_sem,
    s_recv_sem,
    n_send_sem,
    n_recv_sem,
    a_send_sem,
    a_recv_sem,
    rs_recv_sem,
    local_sem,
):
    Z, X, M = sizes
    H = Z // 2
    tokens = q_ref.shape[0]
    group = q_ref.shape[1] // HD
    req, m = lax.axis_index("req"), lax.axis_index("mp")
    z, x = req // X, req % X
    right = {"req": ((z + 1) % Z) * X + x}
    left = {"req": ((z + Z - 1) % Z) * X + x}
    toward = (right, left)

    def x_peer(i):
        return {"req": z * X + (x + i) % X}

    def m_peer(i):
        return {"mp": (m + i) % M}

    def remote(src, dst, send_sem, recv_sem, device):
        return pltpu.make_async_remote_copy(
            src_ref=src,
            dst_ref=dst,
            send_sem=send_sem,
            recv_sem=recv_sem,
            device_id=device,
            device_id_type=pl.DeviceIdType.MESH,
        )

    def gather_hop(way, kind, half, hop):
        lane = way
        if way == LEFT and kind == VALUE:
            lane = 1 - hop // H
        span = pl.ds(half * BLOCK, BLOCK)
        return remote(
            slab.at[way, hop - 1, kind, span],
            slab.at[lane, hop, kind, span],
            ring_send_sem.at[way, hop % 2, 2 * kind + half],
            ag_recv_sem.at[way, hop, 2 * kind + half],
            toward[way],
        )

    def last_hop(way, kind):
        return H if way == kind else H - 1

    def q_copy(i):
        return remote(
            q_ref, queries.at[x], q_send_sem.at[i], q_recv_sem.at[i], x_peer(i)
        )

    def g_copy(i):
        return remote(
            heads_grad.at[x], heads_grad.at[x], g_send_sem.at[i], g_recv_sem.at[i], x_peer(i)
        )

    def h_copy(i):
        return remote(
            hg_send.at[i], hg_recv.at[i], h_send_sem.at[i], h_recv_sem.at[i], m_peer(i)
        )

    def s_copy(i):
        return remote(stat_send, stat_recv.at[i], s_send_sem.at[i], s_recv_sem.at[i], x_peer(i))

    def n_copy(i):
        return remote(
            num_send.at[(x + i) % X], num_recv.at[i], n_send_sem.at[i], n_recv_sem.at[i], x_peer(i)
        )

    def a_copy(i):
        return remote(heads.at[m], heads.at[m], a_send_sem.at[i], a_recv_sem.at[i], m_peer(i))

    def ring_hop(way, kind, half, dist):
        span = pl.ds(half * BLOCK, BLOCK)
        return remote(
            ring_send.at[way, dist, kind, span],
            ring_recv.at[way, dist - 1, kind, span],
            ring_send_sem.at[way, dist % 2, 2 * kind + half],
            rs_recv_sem.at[way, dist, 2 * kind + half],
            toward[way],
        )

    w_copy = pltpu.make_async_copy(w_hbm, w_ref, local_sem.at[0])
    og_copy = pltpu.make_async_copy(og_hbm, og_ref, local_sem.at[1])
    table_copy = pltpu.make_async_copy(codes, table, local_sem.at[2])
    attn_copy = pltpu.make_async_copy(attn_ref, attn_hbm, local_sem.at[3])
    og_copy.start()
    w_copy.start()
    barrier = pltpu.get_barrier_semaphore()
    partners = [right, left] + [x_peer(i) for i in range(1, X)] + [m_peer(i) for i in range(1, M)]
    for partner in partners:
        pl.semaphore_signal(
            barrier, inc=1, device_id=partner, device_id_type=pl.DeviceIdType.MESH
        )
    for kind in (KEY, VALUE):
        own = bank_ref[pl.ds(kind, 2 * BLOCK, stride=2), :].astype(jnp.bfloat16)
        slab[RIGHT, 0, kind] = own
        slab[LEFT, 0, kind] = own
        slab[LEFT, H, kind] = own
    queries[x] = q_ref[...]
    pl.semaphore_wait(barrier, len(partners))

    near = [i for i in range(1, X) if i in (1, X - 1)]
    far = [i for i in range(1, X) if i not in near]
    order = [0] + near + far
    for kind in (KEY, VALUE):
        for half in range(2):
            for way in (RIGHT, LEFT):
                gather_hop(way, kind, half, 1).start()
    for i in order[1:]:
        q_copy(i).start()

    og_copy.wait()
    og = og_ref[...].T
    w_copy.wait()

    def share(i):
        target = (m + i) % M
        band = pl.ds(pl.multiple_of(target * (group * HD), group * HD), group * HD)
        hg_send[i] = dot(og, w_ref[:, band], NN).astype(jnp.bfloat16)

    for i in range(1, M):
        share(i)
        h_copy(i).start()
    share(0)

    numer[...] = jnp.zeros_like(numer)
    denom[...] = jnp.zeros_like(denom)
    key_pos = lax.broadcasted_iota(jnp.int32, (tokens, tokens), 0)
    query_pos = lax.broadcasted_iota(jnp.int32, (tokens, tokens), 1)
    causal = key_pos <= query_pos
    for g in range(group):
        lanes = slice(g * HD, (g + 1) * HD)
        score = dot(k_ref[...], q_ref[:, lanes], NT)
        exp = jnp.exp(softcap * jnp.tanh(score * (qscale / softcap)))
        exp = jnp.where(causal, exp, 0.0)
        denom[x, g : g + 1, :] = jnp.sum(exp, axis=0, keepdims=True)
        numer[x, lanes, :] = dot(v_ref[...], exp.astype(jnp.bfloat16), TN)

    lists = lists_ref[...]
    request_lane = lax.broadcasted_iota(jnp.int32, lists.shape, 1)
    wide = (lists.shape[0], HD)
    entry = lax.broadcasted_iota(jnp.int32, wide, 0)
    lane = lax.broadcasted_iota(jnp.int32, wide, 1)
    is_ahead = lane >= AHEAD
    place = jnp.where(is_ahead, lane - AHEAD, lane)
    spot = jnp.where(is_ahead, jnp.where(place == H, z, z + place), z - place + Z)
    spot = jnp.where(spot >= Z, spot - Z, spot)
    owner = spot * X + x
    for r in range(X):
        column = jnp.sum(
            jnp.where(request_lane == z * X + r, lists, 0), axis=1, keepdims=True
        )
        hit = (entry < block_count[z * X + r]) & (lax.shift_right_logical(column, 1) == owner)
        codes[r : r + 1, :] = jnp.sum(
            jnp.where(hit, 1 + (column & 1), 0), axis=0, keepdims=True
        )
    table_copy.start()
    table_copy.wait()

    def pick(code, way, step, kind):
        return choose(
            code == 2, slab[way, step, kind, BLOCK:, :], slab[way, step, kind, :BLOCK, :]
        )

    def join(pieces):
        return pieces[0] if len(pieces) == 1 else jnp.concatenate(pieces, axis=0)

    def forward(step, offsets, sides=(0, 1)):
        covered = slice(sides[0] * BLOCK, (sides[-1] + 1) * BLOCK)
        for offset in offsets:
            r = (x + offset) % X
            taken = [table[r, side * AHEAD + step] for side in sides]
            keys = join([pick(code, side, step, KEY) for side, code in zip(sides, taken)])
            chosen = [pick(code, side, step, VALUE) for side, code in zip(sides, taken)]
            vals = join(
                [choose(code > 0, val, jnp.zeros_like(val)) for val, code in zip(chosen, taken)]
            )
            halves = []
            for g in range(group):
                lanes = slice(g * HD, (g + 1) * HD)
                tanh = jnp.tanh(dot(keys, queries[r, :, lanes], NT) * (qscale / softcap))
                exp = jnp.exp(softcap * tanh)
                half = exp.astype(jnp.bfloat16)
                halves.append(half)
                exps[step - 1, r, g, covered, :] = half
                slopes[step - 1, r, g, covered, :] = (exp * (1.0 - tanh * tanh)).astype(
                    jnp.bfloat16
                )
                added = denom[r, g : g + 1, :]
                for i, code in enumerate(taken):
                    mine = jnp.sum(exp[i * BLOCK : (i + 1) * BLOCK], axis=0, keepdims=True)
                    added += choose(code > 0, mine, jnp.zeros_like(mine))
                denom[r, g : g + 1, :] = added
            mixed = dot(vals, jnp.concatenate(halves, axis=1), TN)
            for g in range(group):
                numer[r, g * HD : (g + 1) * HD, :] += mixed[:, g * tokens : (g + 1) * tokens]

    live = lax.broadcasted_iota(jnp.int32, (group * HD, tokens), 1) < token_count[0]
    early, late = order[: X // 2], order[X // 2 :]

    def pass_on(step, kind):
        for half in range(2):
            for way in (RIGHT, LEFT):
                last = last_hop(way, kind)

                @pl.when(step <= last)
                def _():
                    gather_hop(way, kind, half, step).wait_recv()

                @pl.when((step < last) & (step > 1))
                def _():
                    gather_hop(way, kind, half, step - 1).wait_send()

                @pl.when(step < last)
                def _():
                    gather_hop(way, kind, half, step + 1).start()

    def gather_step(step, carry):
        @pl.when(step <= H)
        def _():
            pass_on(step, KEY)

        @pl.when(step == 2)
        def _():
            for i in late:
                q_copy(X - i).wait_recv()

        @pl.when((step > 1) & (step <= H))
        def _():
            forward(step - 1, late)

        @pl.when(step == H + 1)
        def _():
            forward(H, late, (0,))

        @pl.when(step <= H)
        def _():
            pass_on(step, VALUE)

        @pl.when(step == 1)
        def _():
            for i in early[1:]:
                q_copy(X - i).wait_recv()

        @pl.when(step < H)
        def _():
            forward(step, early)

        @pl.when(step == H)
        def _():
            forward(H, early, (0,))

        @pl.when(step == max(2, H // 2 - 1))
        def _():
            forward(H, early, (1,))

        @pl.when(step == max(2, H // 2))
        def _():
            forward(H, late, (1,))

        @pl.when(step == min(6, H))
        def _():
            total = hg_send[0].astype(jnp.float32)
            for i in range(1, M):
                h_copy(i).wait_recv()
                total += hg_recv[i].astype(jnp.float32)
            heads_grad[x] = jnp.where(live, total.T, 0.0).astype(jnp.bfloat16)
            for i in order[1:]:
                g_copy(i).start()

        return carry

    lax.fori_loop(1, H + 2, gather_step, 0)

    for i in range(1, X):
        g_copy(i).wait_recv()
    for r in range(X):
        for g in range(group):
            lanes = slice(g * HD, (g + 1) * HD)
            row = (r * group + g) * 2
            stat_send[row : row + 1, :] = denom[r, g : g + 1, :]
            stat_send[row + 1 : row + 2, :] = jnp.sum(
                heads_grad[r, lanes, :].astype(jnp.float32) * numer[r, lanes, :],
                axis=0,
                keepdims=True,
            )
    for i in order[1:]:
        s_copy(i).start()
    num_send[...] = numer[...].astype(jnp.bfloat16)
    for i in order[1:]:
        n_copy(i).start()
    ring_recv[RIGHT, H - 1, VALUE] = jnp.zeros_like(ring_recv[RIGHT, H - 1, VALUE])
    ring_recv[LEFT, H - 1, KEY] = jnp.zeros_like(ring_recv[LEFT, H - 1, KEY])
    for kind in (KEY, VALUE):
        for way in (RIGHT, LEFT):
            last = last_hop(way, kind)
            for hop in range(max(1, last - 1), last + 1):
                for half in range(2):
                    gather_hop(way, kind, half, hop).wait_send()
    for i in range(1, X):
        q_copy(i).wait_send()
        g_copy(i).wait_send()
    for i in range(1, M):
        h_copy(i).wait_send()
    for r in range(X):
        vals = join([pick(table[r, side * AHEAD + H], side, H, VALUE) for side in range(2)])
        for g in range(group):
            first_prob[r, g] = dot(vals, heads_grad[r, g * HD : (g + 1) * HD, :], NN)
    stats = stat_send[...]
    for i in range(1, X):
        s_copy(i).wait_recv()
        stats += stat_recv[i]
    for r in range(X):
        for g in range(group):
            lanes = slice(g * HD, (g + 1) * HD)
            row = (r * group + g) * 2
            inverse = 1.0 / stats[row : row + 1, :]
            rows[r, 2 * g : 2 * g + 1, :] = inverse
            rows[r, 2 * g + 1 : 2 * g + 2, :] = inverse * stats[row + 1 : row + 2, :]
            scaled_grad[r, lanes, :] = (
                heads_grad[r, lanes, :].astype(jnp.float32) * inverse
            ).astype(jnp.bfloat16)

    def backward(dist, requests, first, known=False):
        slot = dist % 2
        found = []
        for r in requests:
            code_a, code_b = table[r, dist], table[r, AHEAD + dist]
            vals = None
            if not known:
                vals = join([pick(code_a, 0, dist, VALUE), pick(code_b, 1, dist, VALUE)])
            key_grad = jnp.zeros((2 * BLOCK, HD), jnp.float32)
            value_grad = jnp.zeros((2 * BLOCK, HD), jnp.float32)
            for g in range(group):
                lanes = slice(g * HD, (g + 1) * HD)
                inverse = rows[r, 2 * g : 2 * g + 1, :]
                delta = rows[r, 2 * g + 1 : 2 * g + 2, :]
                if known:
                    dprob = first_prob[r, g]
                else:
                    dprob = dot(vals, heads_grad[r, lanes, :], NN)
                slope = slopes[dist - 1, r, g].astype(jnp.float32)
                dscore = slope * ((dprob - delta) * (inverse * qscale))
                key_grad += dot(dscore.astype(jnp.bfloat16), queries[r, :, lanes], NN)
                value_grad += dot(exps[dist - 1, r, g], scaled_grad[r, lanes, :], NT)
            found.append(((code_a, code_b), (key_grad, value_grad)))
        none = jnp.zeros((BLOCK, HD), jnp.float32)
        for side in range(2):
            span = slice(side * BLOCK, (side + 1) * BLOCK)
            for kind in (KEY, VALUE):
                for block in range(2):
                    place = slice(block * BLOCK, (block + 1) * BLOCK)
                    total = none if first else part[slot, side, kind, place, :]
                    for codes, grads in found:
                        total += choose(codes[side] == block + 1, grads[kind][span], none)
                    part[slot, side, kind, place, :] = total

    def hand_over(dist, kind):
        slot = dist % 2
        for half in range(2):
            span = slice(half * BLOCK, (half + 1) * BLOCK)
            for way in (RIGHT, LEFT):
                last = last_hop(way, kind)
                side = 1 - way

                @pl.when(dist == H)
                def _():
                    if way == kind:
                        ring_send[way, H, kind, span, :] = part[slot, 0, kind, span, :].astype(
                            jnp.bfloat16
                        )
                        ring_hop(way, kind, half, H).start()

                @pl.when(dist < H)
                def _():
                    @pl.when(dist < last)
                    def _():
                        ring_hop(way, kind, half, dist + 1).wait_recv()

                    ring_send[way, dist, kind, span, :] = (
                        part[slot, side, kind, span, :]
                        + ring_recv[way, dist, kind, span, :].astype(jnp.float32)
                    ).astype(jnp.bfloat16)

                    @pl.when(dist + 2 <= last)
                    def _():
                        ring_hop(way, kind, half, dist + 2).wait_send()

                    ring_hop(way, kind, half, dist).start()

    def scatter_step(index, carry):
        dist = H + 1 - index

        hand_over(dist, KEY)

        @pl.when(dist > 1)
        def _():
            backward(dist - 1, range(X // 2), True)

        hand_over(dist, VALUE)

        @pl.when(dist > 1)
        def _():
            backward(dist - 1, range(X // 2, X), False)

        @pl.when(index == min(4, H))
        def _():
            total = numer[x]
            for i in range(1, X):
                n_copy(i).wait_recv()
                total += num_recv[i].astype(jnp.float32)
            out = jnp.concatenate(
                [total[g * HD : (g + 1) * HD] * rows[x, 2 * g : 2 * g + 1, :] for g in range(group)],
                axis=0,
            )
            heads[m] = jnp.where(live, out, 0.0).astype(jnp.bfloat16)
            for i in range(1, M):
                a_copy(i).start()

        return carry

    backward(H, range(X), True, known=True)
    own_sum[...] = part[H % 2, 1]
    lax.fori_loop(1, H + 1, scatter_step, 0)

    for i in range(1, M):
        a_copy(i).wait_recv()
    depth = group * HD
    total = dot(w_ref[:, :depth], heads[0], NN)
    for j in range(1, M):
        total += dot(w_ref[:, j * depth : (j + 1) * depth], heads[j], NN)
    attn_ref[...] = total
    attn_copy.start()
    for i in range(1, X):
        s_copy(i).wait_send()
        n_copy(i).wait_send()
    for i in range(1, M):
        a_copy(i).wait_send()

    for kind in (KEY, VALUE):
        for half in range(2):
            for way in (RIGHT, LEFT):
                ring_hop(way, kind, half, 1).wait_recv()
        total = own_sum[kind]
        for way in (RIGHT, LEFT):
            total += ring_recv[way, 0, kind].astype(jnp.float32)
        grad_ref[pl.ds(kind, 2 * BLOCK, stride=2), :] = total

    for kind in (KEY, VALUE):
        for way in (RIGHT, LEFT):
            for dist in range(1, min(2, last_hop(way, kind)) + 1):
                for half in range(2):
                    ring_hop(way, kind, half, dist).wait_send()
    attn_copy.wait()


def update_kernel(
    grad_ref,
    bank_ref,
    one_ref,
    two_ref,
    attn_ref,
    attn_out,
    bank_out,
    one_out,
    two_out,
):
    attn_out[...] = attn_ref[...]
    grad = grad_ref[...]
    moment_next = beta_one * one_ref[...] + (1.0 - beta_one) * grad
    second_next = beta_two * two_ref[...] + (1.0 - beta_two) * grad * grad
    one_out[...] = moment_next
    two_out[...] = second_next
    bank_out[...] = bank_ref[...] - learn_rate * (moment_next / bias_one) / (
        jnp.sqrt(second_next / bias_two) + adam_eps
    )


def local(
    Z,
    X,
    queries,
    keys,
    values,
    out_weight,
    out_grad,
    bank,
    moment_one,
    moment_two,
    block_list,
    block_count,
    token_count,
):
    M = lax.axis_size("mp")
    H = Z // 2
    tokens, heads_width = queries.shape
    group = heads_width // HD
    width = out_weight.shape[1]

    flat = (2 * bank.shape[0], HD)
    bf16, f32 = jnp.bfloat16, jnp.float32
    rows_local = bank.shape[0]
    vmem = pltpu.VMEM
    dma = pltpu.SemaphoreType.DMA
    smem_spec = pl.BlockSpec(memory_space=pltpu.SMEM)
    vmem_spec = pl.BlockSpec(memory_space=pltpu.VMEM)
    any_spec = pl.BlockSpec(memory_space=pl.ANY)
    attn_out, grad = pl.pallas_call(
        functools.partial(step_kernel, (Z, X, M)),
        out_shape=(
            jax.ShapeDtypeStruct((width, tokens), f32),
            jax.ShapeDtypeStruct(flat, f32),
        ),
        in_specs=[smem_spec, smem_spec] + [vmem_spec] * 5 + [any_spec] * 2,
        out_specs=(any_spec, vmem_spec),
        scratch_shapes=[
            vmem((width, out_weight.shape[0]), bf16),
            vmem((width, tokens), bf16),
            vmem((width, tokens), f32),
            vmem((X, HD), jnp.int32),
            pltpu.SMEM((X, HD), jnp.int32),
            vmem((2, H + 1, 2, rows_local, HD), bf16),
            vmem((X, tokens, heads_width), bf16),
            vmem((X, heads_width, tokens), bf16),
            vmem((X, heads_width, tokens), bf16),
            vmem((H, X, group, 2 * BLOCK, tokens), bf16),
            vmem((H, X, group, 2 * BLOCK, tokens), bf16),
            vmem((X, heads_width, tokens), f32),
            vmem((X, group, tokens), f32),
            vmem((M, tokens, heads_width), bf16),
            vmem((M, tokens, heads_width), bf16),
            vmem((2 * X * group, tokens), f32),
            vmem((X, 2 * X * group, tokens), f32),
            vmem((X, 2 * group, tokens), f32),
            vmem((X, heads_width, tokens), bf16),
            vmem((X, heads_width, tokens), bf16),
            vmem((M, heads_width, tokens), bf16),
            vmem((2, 2, 2, rows_local, HD), f32),
            vmem((2, rows_local, HD), f32),
            vmem((X, group, 2 * BLOCK, tokens), f32),
            vmem((2, H + 1, 2, rows_local, HD), bf16),
            vmem((2, H + 1, 2, rows_local, HD), bf16),
            dma((2, 2, 4)),
            dma((2, H + 1, 4)),
            dma((X,)),
            dma((X,)),
            dma((X,)),
            dma((X,)),
            dma((M,)),
            dma((M,)),
            dma((X,)),
            dma((X,)),
            dma((X,)),
            dma((X,)),
            dma((M,)),
            dma((M,)),
            dma((2, H + 1, 4)),
            dma((4,)),
        ],
        compiler_params=pltpu.CompilerParams(
            collective_id=0, has_side_effects=True, vmem_limit_bytes=56 << 20
        ),
    )(
        block_count,
        token_count,
        block_list.T,
        bank.reshape(flat),
        queries,
        keys,
        values,
        out_weight.T,
        out_grad.T,
    )


    def half_rows(rows, columns):
        return pl.BlockSpec((rows // 2, columns), lambda i: (i, 0))

    attn_out, bank_next, moment_next, second_next = pl.pallas_call(
        update_kernel,
        out_shape=(jax.ShapeDtypeStruct((width, tokens), f32),)
        + (jax.ShapeDtypeStruct(flat, f32),) * 3,
        grid=(2,),
        in_specs=[half_rows(*flat)] * 4 + [half_rows(width, tokens)],
        out_specs=(half_rows(width, tokens),) + (half_rows(*flat),) * 3,
    )(grad, bank.reshape(flat), moment_one.reshape(flat), moment_two.reshape(flat), attn_out)
    return (
        attn_out.T,
        bank_next.reshape(bank.shape),
        moment_next.reshape(bank.shape),
        second_next.reshape(bank.shape),
    )


def solution(mesh):
    reqs = mesh.shape["req"]
    X = 4 if reqs >= 64 else 2
    return jax.shard_map(
        functools.partial(local, reqs // X, X),
        mesh=mesh,
        in_specs=(
            P("req", "mp"),
            P("req", "mp"),
            P("req", "mp"),
            P(None, "mp"),
            P("req", "mp"),
            P("req", None, "mp"),
            P("req", None, "mp"),
            P("req", None, "mp"),
            P(),
            P(),
            P("req"),
        ),
        out_specs=(
            P("req", "mp"),
            P("req", None, "mp"),
            P("req", None, "mp"),
            P("req", None, "mp"),
        ),
        check_vma=False,
    )
```

```python
import functools

import jax
import jax.numpy as jnp
from jax import lax
from jax.experimental import pallas as pl
from jax.experimental.pallas import tpu as pltpu
from jax.sharding import PartitionSpec as P

HD = 128
BLOCK = 128
KEY, VALUE = 0, 1
RIGHT, LEFT = 0, 1
AHEAD = 64

softcap = 50.0
qscale = 1.0 / 12.0
beta_one = 0.9
beta_two = 0.999
learn_rate = 0.3
adam_eps = 1e-08
bias_one = 1.0 - 0.9**10
bias_two = 1.0 - 0.999**10

NN = (((1,), (0,)), ((), ()))
NT = (((1,), (1,)), ((), ()))
TN = (((0,), (0,)), ((), ()))


def dot(a, b, dims):
    return lax.dot_general(a, b, dims, preferred_element_type=jnp.float32)


def choose(flag, a, b):
    return lax.select(flag, a, b)


def step_kernel(
    sizes,
    block_count,
    token_count,
    lists_ref,
    bank_ref,
    q_ref,
    k_ref,
    v_ref,
    w_hbm,
    og_hbm,
    attn_hbm,
    grad_ref,
    w_ref,
    og_ref,
    attn_ref,
    codes,
    table,
    slab,
    queries,
    heads_grad,
    scaled_grad,
    exps,
    slopes,
    numer,
    denom,
    hg_send,
    hg_recv,
    stat_send,
    stat_recv,
    rows,
    num_send,
    num_recv,
    heads,
    part,
    own_sum,
    first_prob,
    ring_send,
    ring_recv,
    ring_send_sem,
    ag_recv_sem,
    q_send_sem,
    q_recv_sem,
    g_send_sem,
    g_recv_sem,
    h_send_sem,
    h_recv_sem,
    s_send_sem,
    s_recv_sem,
    n_send_sem,
    n_recv_sem,
    a_send_sem,
    a_recv_sem,
    rs_recv_sem,
    local_sem,
):
    Z, X, M = sizes
    H = Z // 2
    tokens = q_ref.shape[0]
    group = q_ref.shape[1] // HD
    req, m = lax.axis_index("req"), lax.axis_index("mp")
    z, x = req // X, req % X
    right = {"req": ((z + 1) % Z) * X + x}
    left = {"req": ((z + Z - 1) % Z) * X + x}
    toward = (right, left)

    def x_peer(i):
        return {"req": z * X + (x + i) % X}

    def m_peer(i):
        return {"mp": (m + i) % M}

    def remote(src, dst, send_sem, recv_sem, device):
        return pltpu.make_async_remote_copy(
            src_ref=src,
            dst_ref=dst,
            send_sem=send_sem,
            recv_sem=recv_sem,
            device_id=device,
            device_id_type=pl.DeviceIdType.MESH,
        )

    def gather_hop(way, kind, half, hop):
        lane = way
        if way == LEFT and kind == VALUE:
            lane = 1 - hop // H
        span = pl.ds(half * BLOCK, BLOCK)
        return remote(
            slab.at[way, hop - 1, kind, span],
            slab.at[lane, hop, kind, span],
            ring_send_sem.at[way, hop % 2, 2 * kind + half],
            ag_recv_sem.at[way, hop, 2 * kind + half],
            toward[way],
        )

    def last_hop(way, kind):
        return H if way == kind else H - 1

    def q_copy(i):
        return remote(
            q_ref, queries.at[x], q_send_sem.at[i], q_recv_sem.at[i], x_peer(i)
        )

    def g_copy(i):
        return remote(
            heads_grad.at[x], heads_grad.at[x], g_send_sem.at[i], g_recv_sem.at[i], x_peer(i)
        )

    def h_copy(i):
        return remote(
            hg_send.at[i], hg_recv.at[i], h_send_sem.at[i], h_recv_sem.at[i], m_peer(i)
        )

    def s_copy(i):
        return remote(stat_send, stat_recv.at[i], s_send_sem.at[i], s_recv_sem.at[i], x_peer(i))

    def n_copy(i):
        return remote(
            num_send.at[(x + i) % X], num_recv.at[i], n_send_sem.at[i], n_recv_sem.at[i], x_peer(i)
        )

    def a_copy(i):
        return remote(heads.at[m], heads.at[m], a_send_sem.at[i], a_recv_sem.at[i], m_peer(i))

    def ring_hop(way, kind, half, dist):
        span = pl.ds(half * BLOCK, BLOCK)
        return remote(
            ring_send.at[way, dist, kind, span],
            ring_recv.at[way, dist - 1, kind, span],
            ring_send_sem.at[way, dist % 2, 2 * kind + half],
            rs_recv_sem.at[way, dist, 2 * kind + half],
            toward[way],
        )

    w_copy = pltpu.make_async_copy(w_hbm, w_ref, local_sem.at[0])
    og_copy = pltpu.make_async_copy(og_hbm, og_ref, local_sem.at[1])
    table_copy = pltpu.make_async_copy(codes, table, local_sem.at[2])
    attn_copy = pltpu.make_async_copy(attn_ref, attn_hbm, local_sem.at[3])
    og_copy.start()
    w_copy.start()
    barrier = pltpu.get_barrier_semaphore()
    partners = [right, left] + [x_peer(i) for i in range(1, X)] + [m_peer(i) for i in range(1, M)]
    for partner in partners:
        pl.semaphore_signal(
            barrier, inc=1, device_id=partner, device_id_type=pl.DeviceIdType.MESH
        )
    for kind in (KEY, VALUE):
        own = bank_ref[pl.ds(kind, 2 * BLOCK, stride=2), :].astype(jnp.bfloat16)
        slab[RIGHT, 0, kind] = own
        slab[LEFT, 0, kind] = own
        slab[LEFT, H, kind] = own
    queries[x] = q_ref[...]
    pl.semaphore_wait(barrier, len(partners))

    near = [i for i in range(1, X) if i in (1, X - 1)]
    far = [i for i in range(1, X) if i not in near]
    order = [0] + near + far
    for kind in (KEY, VALUE):
        for half in range(2):
            for way in (RIGHT, LEFT):
                gather_hop(way, kind, half, 1).start()
    for i in order[1:]:
        q_copy(i).start()

    og_copy.wait()
    og = og_ref[...].T
    w_copy.wait()

    def share(i):
        target = (m + i) % M
        band = pl.ds(pl.multiple_of(target * (group * HD), group * HD), group * HD)
        hg_send[i] = dot(og, w_ref[:, band], NN).astype(jnp.bfloat16)

    for i in range(1, M):
        share(i)
        h_copy(i).start()
    share(0)

    numer[...] = jnp.zeros_like(numer)
    denom[...] = jnp.zeros_like(denom)
    key_pos = lax.broadcasted_iota(jnp.int32, (tokens, tokens), 0)
    query_pos = lax.broadcasted_iota(jnp.int32, (tokens, tokens), 1)
    causal = key_pos <= query_pos
    for g in range(group):
        lanes = slice(g * HD, (g + 1) * HD)
        score = dot(k_ref[...], q_ref[:, lanes], NT)
        exp = jnp.exp(softcap * jnp.tanh(score * (qscale / softcap)))
        exp = jnp.where(causal, exp, 0.0)
        denom[x, g : g + 1, :] = jnp.sum(exp, axis=0, keepdims=True)
        numer[x, lanes, :] = dot(v_ref[...], exp.astype(jnp.bfloat16), TN)

    lists = lists_ref[...]
    request_lane = lax.broadcasted_iota(jnp.int32, lists.shape, 1)
    wide = (lists.shape[0], HD)
    entry = lax.broadcasted_iota(jnp.int32, wide, 0)
    lane = lax.broadcasted_iota(jnp.int32, wide, 1)
    is_ahead = lane >= AHEAD
    place = jnp.where(is_ahead, lane - AHEAD, lane)
    spot = jnp.where(is_ahead, jnp.where(place == H, z, z + place), z - place + Z)
    spot = jnp.where(spot >= Z, spot - Z, spot)
    owner = spot * X + x
    for r in range(X):
        column = jnp.sum(
            jnp.where(request_lane == z * X + r, lists, 0), axis=1, keepdims=True
        )
        hit = (entry < block_count[z * X + r]) & (lax.shift_right_logical(column, 1) == owner)
        codes[r : r + 1, :] = jnp.sum(
            jnp.where(hit, 1 + (column & 1), 0), axis=0, keepdims=True
        )
    table_copy.start()
    table_copy.wait()

    def pick(code, way, step, kind):
        return choose(
            code == 2, slab[way, step, kind, BLOCK:, :], slab[way, step, kind, :BLOCK, :]
        )

    def join(pieces):
        return pieces[0] if len(pieces) == 1 else jnp.concatenate(pieces, axis=0)

    def forward(step, offsets, sides=(0, 1)):
        covered = slice(sides[0] * BLOCK, (sides[-1] + 1) * BLOCK)
        for offset in offsets:
            r = (x + offset) % X
            taken = [table[r, side * AHEAD + step] for side in sides]
            keys = join([pick(code, side, step, KEY) for side, code in zip(sides, taken)])
            chosen = [pick(code, side, step, VALUE) for side, code in zip(sides, taken)]
            vals = join(
                [choose(code > 0, val, jnp.zeros_like(val)) for val, code in zip(chosen, taken)]
            )
            halves = []
            for g in range(group):
                lanes = slice(g * HD, (g + 1) * HD)
                tanh = jnp.tanh(dot(keys, queries[r, :, lanes], NT) * (qscale / softcap))
                exp = jnp.exp(softcap * tanh)
                half = exp.astype(jnp.bfloat16)
                halves.append(half)
                exps[step - 1, r, g, covered, :] = half
                slopes[step - 1, r, g, covered, :] = (exp * (1.0 - tanh * tanh)).astype(
                    jnp.bfloat16
                )
                added = denom[r, g : g + 1, :]
                for i, code in enumerate(taken):
                    mine = jnp.sum(exp[i * BLOCK : (i + 1) * BLOCK], axis=0, keepdims=True)
                    added += choose(code > 0, mine, jnp.zeros_like(mine))
                denom[r, g : g + 1, :] = added
            mixed = dot(vals, jnp.concatenate(halves, axis=1), TN)
            for g in range(group):
                numer[r, g * HD : (g + 1) * HD, :] += mixed[:, g * tokens : (g + 1) * tokens]

    live = lax.broadcasted_iota(jnp.int32, (group * HD, tokens), 1) < token_count[0]
    early, late = order[: X // 2], order[X // 2 :]

    def pass_on(step, kind):
        for half in range(2):
            for way in (RIGHT, LEFT):
                last = last_hop(way, kind)

                @pl.when(step <= last)
                def _():
                    gather_hop(way, kind, half, step).wait_recv()

                @pl.when((step < last) & (step > 1))
                def _():
                    gather_hop(way, kind, half, step - 1).wait_send()

                @pl.when(step < last)
                def _():
                    gather_hop(way, kind, half, step + 1).start()

    def gather_step(step, carry):
        @pl.when(step <= H)
        def _():
            pass_on(step, KEY)

        @pl.when(step == 2)
        def _():
            for i in late:
                q_copy(X - i).wait_recv()

        @pl.when((step > 1) & (step <= H))
        def _():
            forward(step - 1, late)

        @pl.when(step == H + 1)
        def _():
            forward(H, late, (0,))

        @pl.when(step <= H)
        def _():
            pass_on(step, VALUE)

        @pl.when(step == 1)
        def _():
            for i in early[1:]:
                q_copy(X - i).wait_recv()

        @pl.when(step < H)
        def _():
            forward(step, early)

        @pl.when(step == H)
        def _():
            forward(H, early, (0,))

        @pl.when(step == max(2, H // 2 - 1))
        def _():
            forward(H, early, (1,))

        @pl.when(step == max(2, H // 2))
        def _():
            forward(H, late, (1,))

        @pl.when(step == min(5, H))
        def _():
            total = hg_send[0].astype(jnp.float32)
            for i in range(1, M):
                h_copy(i).wait_recv()
                total += hg_recv[i].astype(jnp.float32)
            heads_grad[x] = jnp.where(live, total.T, 0.0).astype(jnp.bfloat16)
            for i in order[1:]:
                g_copy(i).start()

        return carry

    lax.fori_loop(1, H + 2, gather_step, 0)

    for i in range(1, X):
        g_copy(i).wait_recv()
    for r in range(X):
        for g in range(group):
            lanes = slice(g * HD, (g + 1) * HD)
            row = (r * group + g) * 2
            stat_send[row : row + 1, :] = denom[r, g : g + 1, :]
            stat_send[row + 1 : row + 2, :] = jnp.sum(
                heads_grad[r, lanes, :].astype(jnp.float32) * numer[r, lanes, :],
                axis=0,
                keepdims=True,
            )
    for i in order[1:]:
        s_copy(i).start()
    num_send[...] = numer[...].astype(jnp.bfloat16)
    for i in order[1:]:
        n_copy(i).start()
    ring_recv[RIGHT, H - 1, VALUE] = jnp.zeros_like(ring_recv[RIGHT, H - 1, VALUE])
    ring_recv[LEFT, H - 1, KEY] = jnp.zeros_like(ring_recv[LEFT, H - 1, KEY])
    for kind in (KEY, VALUE):
        for way in (RIGHT, LEFT):
            last = last_hop(way, kind)
            for hop in range(max(1, last - 1), last + 1):
                for half in range(2):
                    gather_hop(way, kind, half, hop).wait_send()
    for i in range(1, X):
        q_copy(i).wait_send()
        g_copy(i).wait_send()
    for i in range(1, M):
        h_copy(i).wait_send()
    for r in range(X):
        vals = join([pick(table[r, side * AHEAD + H], side, H, VALUE) for side in range(2)])
        for g in range(group):
            first_prob[r, g] = dot(vals, heads_grad[r, g * HD : (g + 1) * HD, :], NN)
    stats = stat_send[...]
    for i in range(1, X):
        s_copy(i).wait_recv()
        stats += stat_recv[i]
    for r in range(X):
        for g in range(group):
            lanes = slice(g * HD, (g + 1) * HD)
            row = (r * group + g) * 2
            inverse = 1.0 / stats[row : row + 1, :]
            rows[r, 2 * g : 2 * g + 1, :] = inverse
            rows[r, 2 * g + 1 : 2 * g + 2, :] = inverse * stats[row + 1 : row + 2, :]
            scaled_grad[r, lanes, :] = (
                heads_grad[r, lanes, :].astype(jnp.float32) * inverse
            ).astype(jnp.bfloat16)

    def backward(dist, requests, first, known=False):
        slot = dist % 2
        found = []
        for r in requests:
            code_a, code_b = table[r, dist], table[r, AHEAD + dist]
            vals = None
            if not known:
                vals = join([pick(code_a, 0, dist, VALUE), pick(code_b, 1, dist, VALUE)])
            key_grad = jnp.zeros((2 * BLOCK, HD), jnp.float32)
            value_grad = jnp.zeros((2 * BLOCK, HD), jnp.float32)
            for g in range(group):
                lanes = slice(g * HD, (g + 1) * HD)
                inverse = rows[r, 2 * g : 2 * g + 1, :]
                delta = rows[r, 2 * g + 1 : 2 * g + 2, :]
                if known:
                    dprob = first_prob[r, g]
                else:
                    dprob = dot(vals, heads_grad[r, lanes, :], NN)
                slope = slopes[dist - 1, r, g].astype(jnp.float32)
                dscore = slope * ((dprob - delta) * (inverse * qscale))
                key_grad += dot(dscore.astype(jnp.bfloat16), queries[r, :, lanes], NN)
                value_grad += dot(exps[dist - 1, r, g], scaled_grad[r, lanes, :], NT)
            found.append(((code_a, code_b), (key_grad, value_grad)))
        none = jnp.zeros((BLOCK, HD), jnp.float32)
        for side in range(2):
            span = slice(side * BLOCK, (side + 1) * BLOCK)
            for kind in (KEY, VALUE):
                for block in range(2):
                    place = slice(block * BLOCK, (block + 1) * BLOCK)
                    total = none if first else part[slot, side, kind, place, :]
                    for codes, grads in found:
                        total += choose(codes[side] == block + 1, grads[kind][span], none)
                    part[slot, side, kind, place, :] = total

    def hand_over(dist, kind):
        slot = dist % 2
        for half in range(2):
            span = slice(half * BLOCK, (half + 1) * BLOCK)
            for way in (RIGHT, LEFT):
                last = last_hop(way, kind)
                side = 1 - way

                @pl.when(dist == H)
                def _():
                    if way == kind:
                        ring_send[way, H, kind, span, :] = part[slot, 0, kind, span, :].astype(
                            jnp.bfloat16
                        )
                        ring_hop(way, kind, half, H).start()

                @pl.when(dist < H)
                def _():
                    @pl.when(dist < last)
                    def _():
                        ring_hop(way, kind, half, dist + 1).wait_recv()

                    ring_send[way, dist, kind, span, :] = (
                        part[slot, side, kind, span, :]
                        + ring_recv[way, dist, kind, span, :].astype(jnp.float32)
                    ).astype(jnp.bfloat16)

                    @pl.when(dist + 2 <= last)
                    def _():
                        ring_hop(way, kind, half, dist + 2).wait_send()

                    ring_hop(way, kind, half, dist).start()

    def scatter_step(index, carry):
        dist = H + 1 - index

        hand_over(dist, KEY)

        @pl.when(dist > 1)
        def _():
            backward(dist - 1, range(X // 2), True)

        hand_over(dist, VALUE)

        @pl.when(dist > 1)
        def _():
            backward(dist - 1, range(X // 2, X), False)

        @pl.when(index == min(4, H))
        def _():
            total = numer[x]
            for i in range(1, X):
                n_copy(i).wait_recv()
                total += num_recv[i].astype(jnp.float32)
            out = jnp.concatenate(
                [total[g * HD : (g + 1) * HD] * rows[x, 2 * g : 2 * g + 1, :] for g in range(group)],
                axis=0,
            )
            heads[m] = jnp.where(live, out, 0.0).astype(jnp.bfloat16)
            for i in range(1, M):
                a_copy(i).start()

        return carry

    backward(H, range(X), True, known=True)
    own_sum[...] = part[H % 2, 1]
    lax.fori_loop(1, H + 1, scatter_step, 0)

    for i in range(1, M):
        a_copy(i).wait_recv()
    depth = group * HD
    total = dot(w_ref[:, :depth], heads[0], NN)
    for j in range(1, M):
        total += dot(w_ref[:, j * depth : (j + 1) * depth], heads[j], NN)
    attn_ref[...] = total
    attn_copy.start()
    for i in range(1, X):
        s_copy(i).wait_send()
        n_copy(i).wait_send()
    for i in range(1, M):
        a_copy(i).wait_send()

    for kind in (KEY, VALUE):
        for half in range(2):
            for way in (RIGHT, LEFT):
                ring_hop(way, kind, half, 1).wait_recv()
        total = own_sum[kind]
        for way in (RIGHT, LEFT):
            total += ring_recv[way, 0, kind].astype(jnp.float32)
        grad_ref[pl.ds(kind, 2 * BLOCK, stride=2), :] = total

    for kind in (KEY, VALUE):
        for way in (RIGHT, LEFT):
            for dist in range(1, min(2, last_hop(way, kind)) + 1):
                for half in range(2):
                    ring_hop(way, kind, half, dist).wait_send()
    attn_copy.wait()


def update_kernel(
    grad_ref,
    bank_ref,
    one_ref,
    two_ref,
    attn_ref,
    attn_out,
    bank_out,
    one_out,
    two_out,
):
    attn_out[...] = attn_ref[...]
    grad = grad_ref[...]
    moment_next = beta_one * one_ref[...] + (1.0 - beta_one) * grad
    second_next = beta_two * two_ref[...] + (1.0 - beta_two) * grad * grad
    one_out[...] = moment_next
    two_out[...] = second_next
    bank_out[...] = bank_ref[...] - learn_rate * (moment_next / bias_one) / (
        jnp.sqrt(second_next / bias_two) + adam_eps
    )


def local(
    Z,
    X,
    queries,
    keys,
    values,
    out_weight,
    out_grad,
    bank,
    moment_one,
    moment_two,
    block_list,
    block_count,
    token_count,
):
    M = lax.axis_size("mp")
    H = Z // 2
    tokens, heads_width = queries.shape
    group = heads_width // HD
    width = out_weight.shape[1]

    flat = (2 * bank.shape[0], HD)
    bf16, f32 = jnp.bfloat16, jnp.float32
    rows_local = bank.shape[0]
    vmem = pltpu.VMEM
    dma = pltpu.SemaphoreType.DMA
    smem_spec = pl.BlockSpec(memory_space=pltpu.SMEM)
    vmem_spec = pl.BlockSpec(memory_space=pltpu.VMEM)
    any_spec = pl.BlockSpec(memory_space=pl.ANY)
    attn_out, grad = pl.pallas_call(
        functools.partial(step_kernel, (Z, X, M)),
        out_shape=(
            jax.ShapeDtypeStruct((width, tokens), f32),
            jax.ShapeDtypeStruct(flat, f32),
        ),
        in_specs=[smem_spec, smem_spec] + [vmem_spec] * 5 + [any_spec] * 2,
        out_specs=(any_spec, vmem_spec),
        scratch_shapes=[
            vmem((width, out_weight.shape[0]), bf16),
            vmem((width, tokens), bf16),
            vmem((width, tokens), f32),
            vmem((X, HD), jnp.int32),
            pltpu.SMEM((X, HD), jnp.int32),
            vmem((2, H + 1, 2, rows_local, HD), bf16),
            vmem((X, tokens, heads_width), bf16),
            vmem((X, heads_width, tokens), bf16),
            vmem((X, heads_width, tokens), bf16),
            vmem((H, X, group, 2 * BLOCK, tokens), bf16),
            vmem((H, X, group, 2 * BLOCK, tokens), bf16),
            vmem((X, heads_width, tokens), f32),
            vmem((X, group, tokens), f32),
            vmem((M, tokens, heads_width), bf16),
            vmem((M, tokens, heads_width), bf16),
            vmem((2 * X * group, tokens), f32),
            vmem((X, 2 * X * group, tokens), f32),
            vmem((X, 2 * group, tokens), f32),
            vmem((X, heads_width, tokens), bf16),
            vmem((X, heads_width, tokens), bf16),
            vmem((M, heads_width, tokens), bf16),
            vmem((2, 2, 2, rows_local, HD), f32),
            vmem((2, rows_local, HD), f32),
            vmem((X, group, 2 * BLOCK, tokens), f32),
            vmem((2, H + 1, 2, rows_local, HD), bf16),
            vmem((2, H + 1, 2, rows_local, HD), bf16),
            dma((2, 2, 4)),
            dma((2, H + 1, 4)),
            dma((X,)),
            dma((X,)),
            dma((X,)),
            dma((X,)),
            dma((M,)),
            dma((M,)),
            dma((X,)),
            dma((X,)),
            dma((X,)),
            dma((X,)),
            dma((M,)),
            dma((M,)),
            dma((2, H + 1, 4)),
            dma((4,)),
        ],
        compiler_params=pltpu.CompilerParams(
            collective_id=0, has_side_effects=True, vmem_limit_bytes=56 << 20
        ),
    )(
        block_count,
        token_count,
        block_list.T,
        bank.reshape(flat),
        queries,
        keys,
        values,
        out_weight.T,
        out_grad.T,
    )


    def half_rows(rows, columns):
        return pl.BlockSpec((rows // 2, columns), lambda i: (i, 0))

    attn_out, bank_next, moment_next, second_next = pl.pallas_call(
        update_kernel,
        out_shape=(jax.ShapeDtypeStruct((width, tokens), f32),)
        + (jax.ShapeDtypeStruct(flat, f32),) * 3,
        grid=(2,),
        in_specs=[half_rows(*flat)] * 4 + [half_rows(width, tokens)],
        out_specs=(half_rows(width, tokens),) + (half_rows(*flat),) * 3,
    )(grad, bank.reshape(flat), moment_one.reshape(flat), moment_two.reshape(flat), attn_out)
    return (
        attn_out.T,
        bank_next.reshape(bank.shape),
        moment_next.reshape(bank.shape),
        second_next.reshape(bank.shape),
    )


def solution(mesh):
    reqs = mesh.shape["req"]
    X = 4 if reqs >= 64 else 2
    return jax.shard_map(
        functools.partial(local, reqs // X, X),
        mesh=mesh,
        in_specs=(
            P("req", "mp"),
            P("req", "mp"),
            P("req", "mp"),
            P(None, "mp"),
            P("req", "mp"),
            P("req", None, "mp"),
            P("req", None, "mp"),
            P("req", None, "mp"),
            P(),
            P(),
            P("req"),
        ),
        out_specs=(
            P("req", "mp"),
            P("req", None, "mp"),
            P("req", None, "mp"),
            P("req", None, "mp"),
        ),
        check_vma=False,
    )
```
